256 devices in a mesh: row: 16 (over z, y_hi), col: 16 (over x, y_lo, core).
Axes of the slice: x: 4, y: 4 (y_hi: 2, y_lo: 2; y = y_hi * 2 + y_lo), z: 8, core: 2. Of those that a mesh axis runs over, the one named last changes fastest.
Arguments:
- pairs: float32 [6400, 6400], P('row', 'col'), may hold values from -6 to 6
- one_body: float32 [80, 80], replicated, may hold values from -0.625 to 0.625
- aux: float32 [80, 80, 512], P('row', 'col'), may hold values from -1 to 1, as said below
- weights: float32 [512], replicated, may hold values from 0.3 to 3
Outputs:
- propagated: float32 [6400, 6400], P('row', 'col')
The draws below stay inside these ranges and needn't reach their ends.
Inputs may be any that keep to these rules, and one draw needn't show every extreme that they name: aux[p, q, a] equals aux[q, p, a].
All inputs are finite; a program needn't handle non-finite values.
Results may differ from the reference program's by a relative error of at most 0.0001.
Values sent between devices are 32-bit elements; how exact they have to be, the bound alone decides.
A program may use at most 64 MiB of HBM per device.

```python
import math
import jax
import jax.numpy as jnp
from jax import lax

N = 80
NAUX = 512
ITERS = 1
PAIRS = 6400


def draw_aux(key, part):
    scale = (NAUX * N * N) ** (-0.25)
    first = jax.random.fold_in(jax.random.fold_in(key, 7), 0)
    values = jnp.clip(jax.random.normal(first, (N, N, NAUX), jnp.float32), -4.0, 4.0)
    values = (values + jnp.transpose(values, (1, 0, 2))) * (scale / 1.4142135)
    values = jnp.clip(values, -1.0, 1.0)
    return values.astype(jnp.float32)


def block_levels(stream_key, shape, pieces, smallest, high):
    gain, own = 1.0, jax.random.fold_in(stream_key, 6)
    for dim, parts in pieces:
        heights = jnp.exp(jax.random.uniform(jax.random.fold_in(own, dim), (parts,), jnp.float32, smallest / len(pieces), high / len(pieces)))
        gain = gain * jnp.repeat(heights, shape[dim] // parts).reshape([-1 if axis == dim else 1 for axis in range(len(shape))])
    return gain


def gaussian(stream_key, shape, width, most, pieces=(), held_as=jnp.bfloat16):
    level = block_levels(stream_key, shape, pieces, -0.22, 0.18) if pieces else 1.0
    array = jax.random.normal(stream_key, shape, jnp.float32) * width * level
    return jnp.minimum(jnp.maximum(array, -most), most).astype(held_as)


def setup_inputs(seed: int = 0) -> dict:
    key_of = jax.random.split(jax.random.key(seed), 5)
    pairs = gaussian(key_of[0], (PAIRS, PAIRS), 1.0, 6.0, ((0, 16), (1, 16)), jnp.float32)
    one_body = gaussian(key_of[1], (N, N), N ** -0.5, 0.625, (), jnp.float32)
    aux = draw_aux(jax.random.fold_in(key_of[4], 71), 0)
    weights = jnp.clip(jnp.exp(jax.random.uniform(key_of[3], (NAUX,), jnp.float32, math.log(0.3), math.log(3.0))), 0.3, 3.0)
    return dict(pairs=pairs, one_body=one_body, aux=aux, weights=weights)


time_step = 0.15
highest = lax.Precision.HIGHEST


def derivative(field, one_body, aux, weights):
    result = jnp.einsum('im,mjkl->ijkl', one_body, field, precision=highest)
    result = result + jnp.einsum('jm,imkl->ijkl', one_body, field, precision=highest)
    result = result - jnp.einsum('ijml,mk->ijkl', field, one_body, precision=highest)
    result = result - jnp.einsum('ijkm,ml->ijkl', field, one_body, precision=highest)
    first_proj = jnp.einsum('ila,ijkl->jka', aux, field, precision=highest) * weights
    second_proj = jnp.einsum('ijkl,jka->ila', field, aux, precision=highest) * weights
    result = result + jnp.einsum('ila,jka->ijkl', aux, first_proj, precision=highest)
    result = result - jnp.einsum('ila,jka->ijkl', second_proj, aux, precision=highest)
    return result


def reference(pairs, one_body, aux, weights):
    field = pairs.reshape(N, N, N, N)
    for step in range(ITERS):
        first = derivative(field, one_body, aux, weights)
        trial = field + time_step * first
        second = derivative(trial, one_body, aux, weights)
        field = field + (time_step / 2.0) * (first + second)
    return field.reshape(N * N, N * N)
```

```python
import functools

import jax
import jax.numpy as jnp
from jax import lax
from jax.experimental import pallas as pl
from jax.experimental.pallas import tpu as pltpu
from jax.sharding import PartitionSpec as P

time_step = 0.15
MESH = pl.DeviceIdType.MESH
F32, BF16 = jnp.float32, jnp.bfloat16
N, G, B, NAUX = 80, 16, 5, 512
NB = N * B
HALF, PART = 208, 104
NN = (((1,), (0,)), ((), ()))
NT = (((1,), (1,)), ((), ()))


def split(x):
    high = x.astype(BF16)
    return high, (x - high.astype(F32)).astype(BF16)


def dot3(ah, al, bh, bl, dims=NN):
    dot = functools.partial(lax.dot_general, dimension_numbers=dims, preferred_element_type=F32)
    return dot(ah, bh) + (dot(ah, bl) + dot(al, bh))


def tile_of(part):
    return pl.ds(pl.multiple_of(16 * lax.rem(part, 5), 16), 16), pl.ds(pl.multiple_of(128 * (part // 5), 128), 128)


def half_piece(z):
    return pl.ds(pl.multiple_of(PART * lax.rem(z, 2), 8), PART), pl.ds(pl.multiple_of(128 * (z // 2), 128), 128)


def piece(member):
    z = member // 2
    return (
        pl.ds(pl.multiple_of(HALF * lax.rem(member, 2) + PART * lax.rem(z, 2), 8), PART),
        pl.ds(pl.multiple_of(128 * (z // 2), 128), 128),
    )


def pack(x_ref, s_ref):
    for i in range(B):
        s_ref[i, :, 0:384] = x_ref[i * N:(i + 1) * N, 0:384]
        for lo, hi in ((0, 8), (8, 10)):
            tail = x_ref[i * N + 8 * lo:i * N + 8 * lo + 8, 384:512]
            for m in range(lo + 1, hi):
                tail = tail + pltpu.roll(x_ref[i * N + 8 * m:i * N + 8 * m + 8, 384:512], 16 * (m - lo), 1)
            s_ref[i, lo:lo + 8, 384:512] = tail


def unpack(u_ref, x_ref):
    lane = lax.broadcasted_iota(jnp.int32, (8, 128), 1)
    for i in range(B):
        x_ref[i * N:(i + 1) * N, 0:384] = u_ref[i, :, 0:384]
        for m in range(10):
            lo = 8 * (m // 8)
            tail = u_ref[i, lo:lo + 8, 384:512]
            if m % 8:
                tail = pltpu.roll(tail, 128 - 16 * (m % 8), 1)
            x_ref[i * N + 8 * m:i * N + 8 * m + 8, 384:512] = jnp.where(lane < 16, tail, 0.0)


def kernel(
    xa_in, xt_in, aux_in, v_ref, bd_ref, h_ref, out_ref,
    xa, xh, xl, th, tl, wide, stage_b, dloc, fsum,
    blh, bll, brh, brl, bdh, bdl, y2h, y2l,
    s_r, s_c, r_r, r_c, o_r, o_c, u_r, u_c,
    a_r, a_c, yp_r, yp_c, pa_r, pa_c, hb_r, hb_c, pb_r, pb_c, yf_r, yf_c,
    local, aux_s, aux_r, fwd_s, fwd_r, bck_s, bck_r, rsa_s, rsa_r, rsb_s, rsb_r, ag_s, ag_r,
):
    me = (lax.axis_index("row"), lax.axis_index("col"))
    s, r, o, u = (s_r, s_c), (r_r, r_c), (o_r, o_c), (u_r, u_c)
    a, yp, pa, hb, pb, yf = (a_r, a_c), (yp_r, yp_c), (pa_r, pa_c), (hb_r, hb_c), (pb_r, pb_c), (yf_r, yf_c)
    partner = tuple(m + 1 - 2 * lax.rem(m, 2) for m in me)

    def at(g, member):
        return (member, me[1]) if g == 0 else (me[0], member)

    def to(g, member, src, dst, ssem, rsem):
        return pltpu.make_async_remote_copy(
            src_ref=src, dst_ref=dst, send_sem=ssem, recv_sem=rsem, device_id=at(g, member), device_id_type=MESH
        )

    def ahead(g, n):
        return lax.rem(me[g] + n, G)

    def behind(g, n):
        return lax.rem(me[g] + G - n, G)

    def loop(lo, hi, body):
        def step(n, carry):
            body(n)
            return carry
        lax.fori_loop(lo, hi, step, 0)

    barrier = pltpu.get_barrier_semaphore()
    for g in range(2):
        loop(1, G, lambda n: pl.semaphore_signal(barrier, inc=1, device_id=at(g, ahead(g, n)), device_id_type=MESH))
    pl.semaphore_wait(barrier, 2 * (G - 1))

    def aux_copy(g, n):
        return to(g, ahead(g, 2 * n), aux_in, a[g].at[me[g]], aux_s.at[g, n], aux_r.at[g, n])

    def aux_relay(g, n):
        src = behind(g, 2 * n)
        block = a[g].at[src]
        return to(g, partner[g], block, block, aux_s.at[g, 8 + n], aux_r.at[g, 8 + n])

    def aux_own(g):
        return to(g, partner[g], aux_in, a[g].at[me[g]], aux_s.at[g, 8], aux_r.at[g, 8])

    def aux_start(g):
        loop(1, 8, lambda n: aux_copy(g, n).start())
        aux_own(g).start()

    def aux_finish(g):
        a[g][me[g]] = aux_in[...]

        def relay(n):
            aux_copy(g, n).wait_recv()
            aux_relay(g, n).start()
        loop(1, 8, relay)
        aux_own(g).wait_recv()
        loop(1, 8, lambda n: aux_relay(g, n).wait_recv())

    def aux_sent(g):
        loop(1, 8, lambda n: aux_copy(g, n).wait_send())
        loop(1, 8, lambda n: aux_relay(g, n).wait_send())
        aux_own(g).wait_send()

    def fwd(g, st, n):
        rows, cols = tile_of(ahead(g, n))
        return to(g, ahead(g, n), s[g].at[:, rows, cols], r[g].at[st, pl.ds(5 * me[g], 5)], fwd_s.at[g, n], fwd_r.at[g, st, n])

    def fwd_own(g, st):
        rows, cols = tile_of(me[g])
        return pltpu.make_async_copy(s[g].at[:, rows, cols], r[g].at[st, pl.ds(5 * me[g], 5)], local.at[g, 0])

    def bck(g, st, n):
        rows, cols = tile_of(me[g])
        return to(g, ahead(g, n), o[g].at[pl.ds(5 * ahead(g, n), 5)], u[g].at[st, :, rows, cols], bck_s.at[g, n], bck_r.at[g, st, n])

    def bck_own(g, st):
        rows, cols = tile_of(me[g])
        return pltpu.make_async_copy(o[g].at[pl.ds(5 * me[g], 5)], u[g].at[st, :, rows, cols], local.at[g, 1])

    def fwd_start(g, st):
        loop(1, G, lambda n: fwd(g, st, n).start())
        fwd_own(g, st).start()

    def fwd_finish(g, st):
        fwd_own(g, st).wait()
        loop(1, G, lambda n: fwd(g, st, n).wait_recv())

    def bck_start(g, st):
        loop(1, G, lambda n: bck(g, st, n).start())
        bck_own(g, st).start()

    def bck_finish(g, st):
        bck_own(g, st).wait()
        loop(1, G, lambda n: bck(g, st, n).wait_recv())

    hh, hl = split(h_ref[0])
    gh, gl = split(h_ref[1])

    def mix(g, st):
        left = (hh, hl) if g == 0 else (gh, gl)
        src = r[g].at[st].reshape(N * 16, 128)
        dst = o[g].reshape(N * 16, 128)
        for w in range(0, 16, 2):
            x = jnp.concatenate([src[pl.ds(w + e, N, stride=16), :] for e in range(2)], axis=1)
            x = dot3(*left, *split(x))
            for e in range(2):
                dst[pl.ds(w + e, N, stride=16), :] = x[:, 128 * e:128 * (e + 1)]

    def rsa(g, st):
        other = pl.multiple_of(HALF * (1 - lax.rem(me[g], 2)), 8)
        return to(g, partner[g], yp[g].at[pl.ds(other, HALF)], pa[g].at[st], rsa_s.at[g], rsa_r.at[g, st])

    def rsb(g, st, n):
        rows, cols = half_piece(ahead(g, 2 * n) // 2)
        return to(g, ahead(g, 2 * n), hb[g].at[rows, cols], pb[g].at[st, n], rsb_s.at[g, n], rsb_r.at[g, st, n])

    def ag(g, st, n):
        block = yf[g].at[st, *piece(me[g])]
        return to(g, ahead(g, 2 * n), block, block, ag_s.at[g, n], ag_r.at[g, st, n])

    def ag_own(g, st):
        block = yf[g].at[st, *piece(me[g])]
        return to(g, partner[g], block, block, ag_s.at[g, 8], ag_r.at[g, st, 8])

    def ag_sent(g, st, n):
        block = yf[g].at[st, *piece(behind(g, 2 * n))]
        return to(g, ahead(g, 2 * n), block, block, ag_s.at[g, n], ag_r.at[g, st, n])

    def ag_relay(g, st, n):
        block = yf[g].at[st, *piece(behind(g, 2 * n))]
        return to(g, partner[g], block, block, ag_s.at[g, 8 + n], ag_r.at[g, st, 8 + n])

    def rsb_start(g, st):
        rsa(g, st).wait_recv()
        keep = pl.multiple_of(HALF * lax.rem(me[g], 2), 8)
        hb[g][...] = yp[g][pl.ds(keep, HALF), :] + pa[g][st]
        loop(1, 8, lambda n: rsb(g, st, n).start())

    def ag_start(g, st):
        loop(1, 8, lambda n: rsb(g, st, n).wait_recv())
        rows, cols = half_piece(me[g] // 2)
        total = hb[g][rows, cols]
        for n in range(1, 8):
            total = total + pb[g][st, n]
        rows, cols = piece(me[g])
        yf[g][st, rows, cols] = total * v_ref[0:1, cols]
        loop(1, 8, lambda n: ag(g, st, n).start())
        ag_own(g, st).start()

    def relay_start(g, st):
        def relay(n):
            ag_sent(g, st, n).wait_recv()
            ag_relay(g, st, n).start()
        loop(1, 8, relay)

    def ag_finish(g, st):
        ag_own(g, st).wait_recv()
        loop(1, 8, lambda n: ag_relay(g, st, n).wait_recv())

    aux_start(1)
    aux_start(0)
    pack(xt_in, s_r)
    pack(xa_in, s_c)
    fwd_start(0, 0)
    fwd_start(1, 0)

    zeros = jnp.zeros((512 - NB, 512), F32)
    wide[NB:512, :] = zeros
    stage_b[NB:512, :] = zeros
    y2h[NB:512, :] = zeros.astype(BF16)
    y2l[NB:512, :] = zeros.astype(BF16)
    for g in range(2):
        yp[g][NB:2 * HALF, :] = zeros[0:2 * HALF - NB]
    bdh[...], bdl[...] = split(bd_ref[...])
    xa[...] = xa_in[...]
    xh[...], xl[...] = split(xa_in[...])
    th[...], tl[...] = split(xt_in[...])

    def gather_left():
        aux_finish(1)
        for c in range(G):
            for i in range(B):
                for t in range(4):
                    stage_b[i * N + 5 * c:i * N + 5 * c + 5, 128 * t:128 * t + 128] = a_c[c, pl.ds(i * 20 + t, 5, stride=4), :]
        blh[...], bll[...] = split(stage_b[...])

    def gather_right():
        aux_finish(0)
        for c in range(G):
            for k in range(B):
                for t in range(4):
                    stage_b[k * N + 5 * c:k * N + 5 * c + 5, 128 * t:128 * t + 128] = a_r[c, pl.ds(k * 4 + t, 5, stride=20), :]
        brh[...], brl[...] = split(stage_b[...])

    def section(st, carry):
        @pl.when(st == 1)
        def _():
            fwd_start(0, st)
            fwd_start(1, st)

        dloc[...] = local_terms()

        @pl.when(st == 0)
        def _():
            gather_left()

        yp_r[0:NB, :] = dot3(xh[...], xl[...], blh[...], bll[...])
        rsa(0, st).start()

        @pl.when(st == 0)
        def _():
            gather_right()

        yp_c[0:NB, :] = dot3(th[...], tl[...], brh[...], brl[...])
        rsa(1, st).start()

        fwd_finish(0, st)
        mix(0, st)
        bck_start(0, st)
        rsb_start(0, st)
        fwd_finish(1, st)
        mix(1, st)
        bck_start(1, st)
        rsb_start(1, st)
        ag_start(0, st)
        ag_start(1, st)
        relay_start(1, st)
        relay_start(0, st)
        bck_finish(1, st)
        unpack(u_c.at[st], wide)
        f = dloc[...] + wide[0:NB, :]
        bck_finish(0, st)
        unpack(u_r.at[st], wide)
        dloc[...] = f + jnp.transpose(wide[...])[0:NB, :]
        ag_finish(1, st)
        y2h[0:NB, :], y2l[0:NB, :] = split(yf_c[st, 0:NB, :])
        dloc[...] = dloc[...] - dot3(brh[0:NB, :], brl[0:NB, :], y2h[...], y2l[...], NT)
        ag_finish(0, st)
        f = dloc[...] + dot3(*split(yf_r[st, 0:NB, :]), blh[...], bll[...], NT)

        for g in range(2):
            loop(1, G, lambda n: fwd(g, st, n).wait_send())
            loop(1, G, lambda n: bck(g, st, n).wait_send())
            rsa(g, st).wait_send()
            loop(1, 8, lambda n: rsb(g, st, n).wait_send())
            loop(1, 8, lambda n: ag(g, st, n).wait_send())
            ag_own(g, st).wait_send()
            loop(1, 8, lambda n: ag_relay(g, st, n).wait_send())

        @pl.when(st == 0)
        def _():
            fsum[...] = f
            x = xa_in[...] + time_step * f
            xa[...] = x
            wide[0:NB, :] = x
            xh[...], xl[...] = split(x)
            xa_t = jnp.transpose(wide[...])[0:NB, :]
            stage_b[0:NB, :] = xa_t
            th[...], tl[...] = split(xa_t)
            pack(stage_b, s_r)
            pack(xa, s_c)
            for g in range(2):
                aux_sent(g)

        @pl.when(st == 1)
        def _():
            out_ref[...] = xa_in[...] + time_step / 2.0 * (fsum[...] + f)

        return carry

    def local_terms():
        left = dot3(bdh[0:NB, 0:512], bdl[0:NB, 0:512], *pad_rows())
        return left - dot3(xh[...], xl[...], bdh[...], bdl[...])

    def pad_rows():
        z = jnp.zeros((512 - NB, 512), BF16)
        return jnp.concatenate([xh[...], z], axis=0), jnp.concatenate([xl[...], z], axis=0)

    lax.fori_loop(0, 2, section, 0)


def shards(pairs, one_body, aux, weights):
    x = pairs.reshape(B, N, B, N)
    pad = lambda m: jnp.pad(m.reshape(NB, NB), ((0, 0), (0, 512 - NB)))
    xa = pad(jnp.transpose(x, (2, 1, 0, 3)))
    xt = pad(jnp.transpose(x, (0, 3, 2, 1)))
    auxp = jnp.pad(aux.reshape(100, 128), ((0, 4), (0, 0)))
    bd = jnp.pad(jnp.kron(jnp.eye(B, dtype=F32), one_body), ((0, 512 - NB), (0, 512 - NB)))
    h = jnp.stack([one_body, -one_body.T])
    vmem = pl.BlockSpec(memory_space=pltpu.VMEM)
    f32 = lambda *shape: pltpu.VMEM(shape, F32)
    b16 = lambda *shape: pltpu.VMEM(shape, BF16)
    dma = lambda *shape: pltpu.SemaphoreType.DMA(shape)
    out = pl.pallas_call(
        kernel,
        out_shape=jax.ShapeDtypeStruct((NB, 512), F32),
        in_specs=[vmem] * 6,
        out_specs=vmem,
        scratch_shapes=[
            f32(NB, 512), b16(NB, 512), b16(NB, 512), b16(NB, 512), b16(NB, 512),
            f32(512, 512), f32(512, 512), f32(NB, 512), f32(NB, 512),
            *[b16(512, 512)] * 8,
            *[f32(B, N, 512)] * 2, *[f32(2, N, 16, 128)] * 2, *[f32(N, 16, 128)] * 2, *[f32(2, B, N, 512)] * 2,
            *[f32(G, PART, 128)] * 2, *[f32(2 * HALF, 512)] * 2, *[f32(2, HALF, 512)] * 2, *[f32(HALF, 512)] * 2,
            *[f32(2, 8, PART, 128)] * 2, *[f32(2, 2 * HALF, 512)] * 2,
            dma(2, 2), dma(2, 16), dma(2, 16), dma(2, 16), dma(2, 2, 16), dma(2, 16), dma(2, 2, 16),
            dma(2), dma(2, 2), dma(2, 8), dma(2, 2, 8), dma(2, 16), dma(2, 2, 16),
        ],
        compiler_params=pltpu.CompilerParams(collective_id=0, has_side_effects=True, vmem_limit_bytes=60 * 1024 * 1024),
        name="heun",
    )(xa, xt, auxp, weights.reshape(1, NAUX), bd, h)
    out = out[:, 0:NB].reshape(B, N, B, N)
    return jnp.transpose(out, (2, 1, 0, 3)).reshape(NB, NB)


def solution(mesh):
    in_specs = (P("row", "col"), P(), P("row", "col", None), P())
    out_specs = P("row", "col")
    return jax.shard_map(shards, mesh=mesh, in_specs=in_specs, out_specs=out_specs, check_vma=False)
```

```python
import functools

import jax
import jax.numpy as jnp
from jax import lax
from jax.experimental import pallas as pl
from jax.experimental.pallas import tpu as pltpu
from jax.sharding import PartitionSpec as P

time_step = 0.15
MESH = pl.DeviceIdType.MESH
F32, BF16 = jnp.float32, jnp.bfloat16
N, G, B, NAUX = 80, 16, 5, 512
NB = N * B
HALF, PART = 208, 104
NN = (((1,), (0,)), ((), ()))
NT = (((1,), (1,)), ((), ()))


def split(x):
    high = x.astype(BF16)
    return high, (x - high.astype(F32)).astype(BF16)


def dot3(ah, al, bh, bl, dims=NN):
    dot = functools.partial(lax.dot_general, dimension_numbers=dims, preferred_element_type=F32)
    return dot(ah, bh) + (dot(ah, bl) + dot(al, bh))


def tile_of(part):
    return pl.ds(pl.multiple_of(16 * lax.rem(part, 5), 16), 16), pl.ds(pl.multiple_of(128 * (part // 5), 128), 128)


def half_piece(z):
    return pl.ds(pl.multiple_of(PART * lax.rem(z, 2), 8), PART), pl.ds(pl.multiple_of(128 * (z // 2), 128), 128)


def piece(member):
    z = member // 2
    return (
        pl.ds(pl.multiple_of(HALF * lax.rem(member, 2) + PART * lax.rem(z, 2), 8), PART),
        pl.ds(pl.multiple_of(128 * (z // 2), 128), 128),
    )


def pack(x_ref, s_ref):
    for i in range(B):
        s_ref[i, :, 0:384] = x_ref[i * N:(i + 1) * N, 0:384]
        for lo, hi in ((0, 8), (8, 10)):
            tail = x_ref[i * N + 8 * lo:i * N + 8 * lo + 8, 384:512]
            for m in range(lo + 1, hi):
                tail = tail + pltpu.roll(x_ref[i * N + 8 * m:i * N + 8 * m + 8, 384:512], 16 * (m - lo), 1)
            s_ref[i, lo:lo + 8, 384:512] = tail


def unpack(u_ref, x_ref):
    lane = lax.broadcasted_iota(jnp.int32, (8, 128), 1)
    for i in range(B):
        x_ref[i * N:(i + 1) * N, 0:384] = u_ref[i, :, 0:384]
        for m in range(10):
            lo = 8 * (m // 8)
            tail = u_ref[i, lo:lo + 8, 384:512]
            if m % 8:
                tail = pltpu.roll(tail, 128 - 16 * (m % 8), 1)
            x_ref[i * N + 8 * m:i * N + 8 * m + 8, 384:512] = jnp.where(lane < 16, tail, 0.0)


def kernel(
    x_in, aux_ref, v_in, h_in, out_ref,
    start, aux_in, v_ref, turn,
    xa, xh, xl, th, tl, wide, stage_b, dloc, fsum,
    blh, bll, brh, brl, bdh, bdl, y2h, y2l,
    s_r, s_c, r_r, r_c, o_r, o_c, u_r, u_c,
    a_r, a_c, yp_r, yp_c, pa_r, pa_c, hb_r, hb_c, pb_r, pb_c, yf_r, yf_c,
    local, aux_s, aux_r, fwd_s, fwd_r, bck_s, bck_r, rsa_s, rsa_r, rsb_s, rsb_r, ag_s, ag_r,
):
    me = (lax.axis_index("row"), lax.axis_index("col"))
    s, r, o, u = (s_r, s_c), (r_r, r_c), (o_r, o_c), (u_r, u_c)
    a, yp, pa, hb, pb, yf = (a_r, a_c), (yp_r, yp_c), (pa_r, pa_c), (hb_r, hb_c), (pb_r, pb_c), (yf_r, yf_c)
    partner = tuple(m + 1 - 2 * lax.rem(m, 2) for m in me)

    def at(g, member):
        return (member, me[1]) if g == 0 else (me[0], member)

    def to(g, member, src, dst, ssem, rsem):
        return pltpu.make_async_remote_copy(
            src_ref=src, dst_ref=dst, send_sem=ssem, recv_sem=rsem, device_id=at(g, member), device_id_type=MESH
        )

    def ahead(g, n):
        return lax.rem(me[g] + n, G)

    def behind(g, n):
        return lax.rem(me[g] + G - n, G)

    def loop(lo, hi, body):
        def step(n, carry):
            body(n)
            return carry
        lax.fori_loop(lo, hi, step, 0)

    def enter():
        barrier = pltpu.get_barrier_semaphore()
        for g in range(2):
            loop(1, G, lambda n: pl.semaphore_signal(barrier, inc=1, device_id=at(g, ahead(g, n)), device_id_type=MESH))
        pl.semaphore_wait(barrier, 2 * (G - 1))

    def aux_copy(g, n):
        return to(g, ahead(g, 2 * n), aux_in, a[g].at[me[g]], aux_s.at[g, n], aux_r.at[g, n])

    def aux_relay(g, n):
        src = behind(g, 2 * n)
        block = a[g].at[src]
        return to(g, partner[g], block, block, aux_s.at[g, 8 + n], aux_r.at[g, 8 + n])

    def aux_own(g):
        return to(g, partner[g], aux_in, a[g].at[me[g]], aux_s.at[g, 8], aux_r.at[g, 8])

    def aux_start(g):
        loop(1, 8, lambda n: aux_copy(g, n).start())
        aux_own(g).start()

    def aux_finish(g):
        a[g][me[g]] = aux_in[...]

        def relay(n):
            aux_copy(g, n).wait_recv()
            aux_relay(g, n).start()
        loop(1, 8, relay)
        aux_own(g).wait_recv()
        loop(1, 8, lambda n: aux_relay(g, n).wait_recv())

    def aux_sent(g):
        loop(1, 8, lambda n: aux_copy(g, n).wait_send())
        loop(1, 8, lambda n: aux_relay(g, n).wait_send())
        aux_own(g).wait_send()

    def fwd(g, st, n):
        rows, cols = tile_of(ahead(g, n))
        return to(g, ahead(g, n), s[g].at[:, rows, cols], r[g].at[st, pl.ds(5 * me[g], 5)], fwd_s.at[g, n], fwd_r.at[g, st, n])

    def fwd_own(g, st):
        rows, cols = tile_of(me[g])
        return pltpu.make_async_copy(s[g].at[:, rows, cols], r[g].at[st, pl.ds(5 * me[g], 5)], local.at[g, 0])

    def bck(g, st, n):
        rows, cols = tile_of(me[g])
        return to(g, ahead(g, n), o[g].at[pl.ds(5 * ahead(g, n), 5)], u[g].at[st, :, rows, cols], bck_s.at[g, n], bck_r.at[g, st, n])

    def bck_own(g, st):
        rows, cols = tile_of(me[g])
        return pltpu.make_async_copy(o[g].at[pl.ds(5 * me[g], 5)], u[g].at[st, :, rows, cols], local.at[g, 1])

    def fwd_start(g, st):
        loop(1, G, lambda n: fwd(g, st, n).start())
        fwd_own(g, st).start()

    def fwd_finish(g, st):
        fwd_own(g, st).wait()
        loop(1, G, lambda n: fwd(g, st, n).wait_recv())

    def bck_start(g, st):
        loop(1, G, lambda n: bck(g, st, n).start())
        bck_own(g, st).start()

    def bck_finish(g, st):
        bck_own(g, st).wait()
        loop(1, G, lambda n: bck(g, st, n).wait_recv())

    turn[...] = jnp.zeros((128, 128), F32)
    turn[0:N, 0:N] = h_in[...]
    hh, hl = split(h_in[...])
    gh, gl = split(-jnp.transpose(turn[...])[0:N, 0:N])

    def mix(g, st):
        left = (hh, hl) if g == 0 else (gh, gl)
        src = r[g].at[st].reshape(N * 16, 128)
        dst = o[g].reshape(N * 16, 128)
        for w in range(0, 16, 2):
            x = jnp.concatenate([src[pl.ds(w + e, N, stride=16), :] for e in range(2)], axis=1)
            x = dot3(*left, *split(x))
            for e in range(2):
                dst[pl.ds(w + e, N, stride=16), :] = x[:, 128 * e:128 * (e + 1)]

    def rsa(g, st):
        other = pl.multiple_of(HALF * (1 - lax.rem(me[g], 2)), 8)
        return to(g, partner[g], yp[g].at[pl.ds(other, HALF)], pa[g].at[st], rsa_s.at[g], rsa_r.at[g, st])

    def rsb(g, st, n):
        rows, cols = half_piece(ahead(g, 2 * n) // 2)
        return to(g, ahead(g, 2 * n), hb[g].at[rows, cols], pb[g].at[st, n], rsb_s.at[g, n], rsb_r.at[g, st, n])

    def ag(g, st, n):
        block = yf[g].at[st, *piece(me[g])]
        return to(g, ahead(g, 2 * n), block, block, ag_s.at[g, n], ag_r.at[g, st, n])

    def ag_own(g, st):
        block = yf[g].at[st, *piece(me[g])]
        return to(g, partner[g], block, block, ag_s.at[g, 8], ag_r.at[g, st, 8])

    def ag_sent(g, st, n):
        block = yf[g].at[st, *piece(behind(g, 2 * n))]
        return to(g, ahead(g, 2 * n), block, block, ag_s.at[g, n], ag_r.at[g, st, n])

    def ag_relay(g, st, n):
        block = yf[g].at[st, *piece(behind(g, 2 * n))]
        return to(g, partner[g], block, block, ag_s.at[g, 8 + n], ag_r.at[g, st, 8 + n])

    def rsb_start(g, st):
        rsa(g, st).wait_recv()
        keep = pl.multiple_of(HALF * lax.rem(me[g], 2), 8)
        hb[g][...] = yp[g][pl.ds(keep, HALF), :] + pa[g][st]
        loop(1, 8, lambda n: rsb(g, st, n).start())

    def ag_start(g, st):
        loop(1, 8, lambda n: rsb(g, st, n).wait_recv())
        rows, cols = half_piece(me[g] // 2)
        total = hb[g][rows, cols]
        for n in range(1, 8):
            total = total + pb[g][st, n]
        rows, cols = piece(me[g])
        yf[g][st, rows, cols] = total * v_ref[0:1, cols]
        loop(1, 8, lambda n: ag(g, st, n).start())
        ag_own(g, st).start()

    def relay_start(g, st):
        def relay(n):
            ag_sent(g, st, n).wait_recv()
            ag_relay(g, st, n).start()
        loop(1, 8, relay)

    def ag_finish(g, st):
        ag_own(g, st).wait_recv()
        loop(1, 8, lambda n: ag_relay(g, st, n).wait_recv())

    for p in range(B):
        for t in range(4):
            aux_in[p * 20 + t * B:p * 20 + t * B + B, :] = aux_ref[p, :, 128 * t:128 * t + 128]
    aux_in[100:PART, :] = jnp.zeros((PART - 100, 128), F32)
    enter()
    aux_start(1)
    aux_start(0)
    zeros = jnp.zeros((512 - NB, 512), F32)
    wide[NB:512, :] = zeros
    start[:, 384:512] = jnp.zeros((NB, 128), F32)
    for k in range(B):
        for i in range(B):
            start[k * N:k * N + N, i * N:i * N + N] = x_in[i * N:i * N + N, k * N:k * N + N]
    pack(start, s_c)
    fwd_start(1, 0)
    wide[0:NB, :] = start[...]
    stage_b[...] = jnp.transpose(wide[...])
    pack(stage_b, s_r)
    fwd_start(0, 0)
    th[...], tl[...] = split(stage_b[0:NB, :])
    xh[...], xl[...] = split(start[...])
    stage_b[NB:512, :] = zeros
    y2h[NB:512, :] = zeros.astype(BF16)
    y2l[NB:512, :] = zeros.astype(BF16)
    for g in range(2):
        yp[g][NB:2 * HALF, :] = zeros[0:2 * HALF - NB]
    v_ref[...] = jnp.broadcast_to(v_in[...].reshape(1, NAUX), (8, NAUX))
    bdh[...] = jnp.zeros((512, 512), BF16)
    bdl[...] = jnp.zeros((512, 512), BF16)
    for i in range(B):
        bdh[i * N:i * N + N, i * N:i * N + N] = hh
        bdl[i * N:i * N + N, i * N:i * N + N] = hl

    def gather_left():
        aux_finish(1)
        for c in range(G):
            for i in range(B):
                for t in range(4):
                    stage_b[i * N + 5 * c:i * N + 5 * c + 5, 128 * t:128 * t + 128] = a_c[c, i * 20 + t * 5:i * 20 + t * 5 + 5, :]
        blh[...], bll[...] = split(stage_b[...])

    def gather_right():
        aux_finish(0)
        for c in range(G):
            for k in range(B):
                for t in range(4):
                    stage_b[k * N + 5 * c:k * N + 5 * c + 5, 128 * t:128 * t + 128] = a_r[c, pl.ds(t * 5 + k, 5, stride=20), :]
        brh[...], brl[...] = split(stage_b[...])

    def section(st, carry):
        @pl.when(st == 1)
        def _():
            fwd_start(0, st)
            fwd_start(1, st)

        dloc[...] = local_terms()

        @pl.when(st == 0)
        def _():
            gather_left()

        yp_r[0:NB, :] = dot3(xh[...], xl[...], blh[...], bll[...])
        rsa(0, st).start()

        @pl.when(st == 0)
        def _():
            gather_right()

        yp_c[0:NB, :] = dot3(th[...], tl[...], brh[...], brl[...])
        rsa(1, st).start()

        rsb_start(1, st)
        rsb_start(0, st)
        fwd_finish(1, st)
        mix(1, st)
        bck_start(1, st)
        fwd_finish(0, st)
        mix(0, st)
        bck_start(0, st)
        ag_start(1, st)
        ag_start(0, st)
        relay_start(1, st)
        relay_start(0, st)
        bck_finish(1, st)
        unpack(u_c.at[st], wide)
        f = dloc[...] + wide[0:NB, :]
        bck_finish(0, st)
        unpack(u_r.at[st], wide)
        dloc[...] = f + jnp.transpose(wide[...])[0:NB, :]
        ag_finish(1, st)
        y2h[0:NB, :], y2l[0:NB, :] = split(yf_c[st, 0:NB, :])
        dloc[...] = dloc[...] - dot3(brh[0:NB, :], brl[0:NB, :], y2h[...], y2l[...], NT)
        ag_finish(0, st)
        f = dloc[...] + dot3(*split(yf_r[st, 0:NB, :]), blh[...], bll[...], NT)

        for g in range(2):
            loop(1, G, lambda n: fwd(g, st, n).wait_send())
            loop(1, G, lambda n: bck(g, st, n).wait_send())
            rsa(g, st).wait_send()
            loop(1, 8, lambda n: rsb(g, st, n).wait_send())
            loop(1, 8, lambda n: ag(g, st, n).wait_send())
            ag_own(g, st).wait_send()
            loop(1, 8, lambda n: ag_relay(g, st, n).wait_send())

        @pl.when(st == 0)
        def _():
            fsum[...] = f
            x = start[...] + time_step * f
            xa[...] = x
            wide[0:NB, :] = x
            xh[...], xl[...] = split(x)
            xa_t = jnp.transpose(wide[...])[0:NB, :]
            stage_b[0:NB, :] = xa_t
            th[...], tl[...] = split(xa_t)
            pack(stage_b, s_r)
            pack(xa, s_c)
            for g in range(2):
                aux_sent(g)

        @pl.when(st == 1)
        def _():
            xa[...] = start[...] + time_step / 2.0 * (fsum[...] + f)
            for k in range(B):
                for i in range(B):
                    out_ref[i * N:i * N + N, k * N:k * N + N] = xa[k * N:k * N + N, i * N:i * N + N]

        return carry

    def local_terms():
        left = dot3(bdh[0:NB, 0:512], bdl[0:NB, 0:512], *pad_rows())
        return left - dot3(xh[...], xl[...], bdh[...], bdl[...])

    def pad_rows():
        z = jnp.zeros((512 - NB, 512), BF16)
        return jnp.concatenate([xh[...], z], axis=0), jnp.concatenate([xl[...], z], axis=0)

    lax.fori_loop(0, 2, section, 0)


def shards(pairs, one_body, aux, weights):
    vmem = pl.BlockSpec(memory_space=pltpu.VMEM)
    f32 = lambda *shape: pltpu.VMEM(shape, F32)
    b16 = lambda *shape: pltpu.VMEM(shape, BF16)
    dma = lambda *shape: pltpu.SemaphoreType.DMA(shape)
    return pl.pallas_call(
        kernel,
        out_shape=jax.ShapeDtypeStruct((NB, NB), F32),
        in_specs=[vmem] * 4,
        out_specs=vmem,
        scratch_shapes=[
            f32(NB, 512), f32(PART, 128), f32(8, NAUX), f32(128, 128),
            f32(NB, 512), b16(NB, 512), b16(NB, 512), b16(NB, 512), b16(NB, 512),
            f32(512, 512), f32(512, 512), f32(NB, 512), f32(NB, 512),
            *[b16(512, 512)] * 8,
            *[f32(B, N, 512)] * 2, *[f32(2, N, 16, 128)] * 2, *[f32(N, 16, 128)] * 2, *[f32(2, B, N, 512)] * 2,
            *[f32(G, PART, 128)] * 2, *[f32(2 * HALF, 512)] * 2, *[f32(2, HALF, 512)] * 2, *[f32(HALF, 512)] * 2,
            *[f32(2, 8, PART, 128)] * 2, *[f32(2, 2 * HALF, 512)] * 2,
            dma(2, 2), dma(2, 16), dma(2, 16), dma(2, 16), dma(2, 2, 16), dma(2, 16), dma(2, 2, 16),
            dma(2), dma(2, 2), dma(2, 8), dma(2, 2, 8), dma(2, 16), dma(2, 2, 16),
        ],
        compiler_params=pltpu.CompilerParams(collective_id=0, has_side_effects=True, vmem_limit_bytes=60 * 1024 * 1024),
        name="heun",
    )(pairs, aux, weights, one_body)


def solution(mesh):
    in_specs = (P("row", "col"), P(), P("row", "col", None), P())
    out_specs = P("row", "col")
    return jax.shard_map(shards, mesh=mesh, in_specs=in_specs, out_specs=out_specs, check_vma=False)
```

```python
import functools

import jax
import jax.numpy as jnp
from jax import lax
from jax.experimental import pallas as pl
from jax.experimental.pallas import tpu as pltpu
from jax.sharding import PartitionSpec as P

time_step = 0.15
MESH = pl.DeviceIdType.MESH
F32, BF16 = jnp.float32, jnp.bfloat16
N, G, B, NAUX = 80, 16, 5, 512
NB = N * B
HALF, PART = 208, 104
NN = (((1,), (0,)), ((), ()))
NT = (((1,), (1,)), ((), ()))


def split(x):
    high = x.astype(BF16)
    return high, (x - high.astype(F32)).astype(BF16)


def dot3(ah, al, bh, bl, dims=NN):
    dot = functools.partial(lax.dot_general, dimension_numbers=dims, preferred_element_type=F32)
    return dot(ah, bh) + (dot(ah, bl) + dot(al, bh))


def tile_of(part):
    return pl.ds(pl.multiple_of(16 * lax.rem(part, 5), 16), 16), pl.ds(pl.multiple_of(128 * (part // 5), 128), 128)


def half_piece(z):
    return pl.ds(pl.multiple_of(PART * lax.rem(z, 2), 8), PART), pl.ds(pl.multiple_of(128 * (z // 2), 128), 128)


def piece(member):
    z = member // 2
    return (
        pl.ds(pl.multiple_of(HALF * lax.rem(member, 2) + PART * lax.rem(z, 2), 8), PART),
        pl.ds(pl.multiple_of(128 * (z // 2), 128), 128),
    )


def pack(x_ref, s_ref):
    for i in range(B):
        s_ref[i, :, 0:384] = x_ref[i * N:(i + 1) * N, 0:384]
        for lo, hi in ((0, 8), (8, 10)):
            tail = x_ref[i * N + 8 * lo:i * N + 8 * lo + 8, 384:512]
            for m in range(lo + 1, hi):
                tail = tail + pltpu.roll(x_ref[i * N + 8 * m:i * N + 8 * m + 8, 384:512], 16 * (m - lo), 1)
            s_ref[i, lo:lo + 8, 384:512] = tail


def unpack(u_ref, x_ref):
    lane = lax.broadcasted_iota(jnp.int32, (8, 128), 1)
    for i in range(B):
        x_ref[i * N:(i + 1) * N, 0:384] = u_ref[i, :, 0:384]
        for m in range(10):
            lo = 8 * (m // 8)
            tail = u_ref[i, lo:lo + 8, 384:512]
            if m % 8:
                tail = pltpu.roll(tail, 128 - 16 * (m % 8), 1)
            x_ref[i * N + 8 * m:i * N + 8 * m + 8, 384:512] = jnp.where(lane < 16, tail, 0.0)


def kernel(
    x_in, aux_ref, v_in, h_in, out_ref,
    start, aux_in, v_ref, turn,
    xa, xh, xl, th, tl, wide, stage_b, dloc, fsum,
    blh, bll, brh, brl, bdh, bdl, y2h, y2l,
    s_r, s_c, r_r, r_c, o_r, o_c, u_r, u_c,
    a_r, a_c, yp_r, yp_c, pa_r, pa_c, hb_r, hb_c, pb_r, px, py, sx, yf_r, yf_c,
    local, aux_s, aux_r, fwd_s, fwd_r, bck_s, bck_r, rsa_s, rsa_r, rsb_s, rsb_r, ag_s, ag_r,
):
    me = (lax.axis_index("row"), lax.axis_index("col"))
    s, r, o, u = (s_r, s_c), (r_r, r_c), (o_r, o_c), (u_r, u_c)
    a, yp, pa, hb, pb, yf = (a_r, a_c), (yp_r, yp_c), (pa_r, pa_c), (hb_r, hb_c), (pb_r, None), (yf_r, yf_c)
    partner = tuple(m + 1 - 2 * lax.rem(m, 2) for m in me)

    def at(g, member):
        return (member, me[1]) if g == 0 else (me[0], member)

    def to(g, member, src, dst, ssem, rsem):
        return pltpu.make_async_remote_copy(
            src_ref=src, dst_ref=dst, send_sem=ssem, recv_sem=rsem, device_id=at(g, member), device_id_type=MESH
        )

    def ahead(g, n):
        return lax.rem(me[g] + n, G)

    def behind(g, n):
        return lax.rem(me[g] + G - n, G)

    def loop(lo, hi, body):
        def step(n, carry):
            body(n)
            return carry
        lax.fori_loop(lo, hi, step, 0)

    def enter():
        barrier = pltpu.get_barrier_semaphore()
        for g in range(2):
            loop(1, G, lambda n: pl.semaphore_signal(barrier, inc=1, device_id=at(g, ahead(g, n)), device_id_type=MESH))
        pl.semaphore_wait(barrier, 2 * (G - 1))

    def aux_copy(g, n):
        return to(g, ahead(g, 2 * n), aux_in, a[g].at[me[g]], aux_s.at[g, n], aux_r.at[g, n])

    def aux_relay(g, n):
        src = behind(g, 2 * n)
        block = a[g].at[src]
        return to(g, partner[g], block, block, aux_s.at[g, 8 + n], aux_r.at[g, 8 + n])

    def aux_own(g):
        return to(g, partner[g], aux_in, a[g].at[me[g]], aux_s.at[g, 8], aux_r.at[g, 8])

    def aux_start(g):
        loop(1, 8, lambda n: aux_copy(g, n).start())
        aux_own(g).start()

    def aux_finish(g):
        a[g][me[g]] = aux_in[...]

        def relay(n):
            aux_copy(g, n).wait_recv()
            aux_relay(g, n).start()
        loop(1, 8, relay)
        aux_own(g).wait_recv()
        loop(1, 8, lambda n: aux_relay(g, n).wait_recv())

    def aux_sent(g):
        loop(1, 8, lambda n: aux_copy(g, n).wait_send())
        loop(1, 8, lambda n: aux_relay(g, n).wait_send())
        aux_own(g).wait_send()

    def fwd(g, st, n):
        rows, cols = tile_of(ahead(g, n))
        return to(g, ahead(g, n), s[g].at[:, rows, cols], r[g].at[st, pl.ds(5 * me[g], 5)], fwd_s.at[g, n], fwd_r.at[g, st, n])

    def fwd_own(g, st):
        rows, cols = tile_of(me[g])
        return pltpu.make_async_copy(s[g].at[:, rows, cols], r[g].at[st, pl.ds(5 * me[g], 5)], local.at[g, 0])

    def bck(g, st, n):
        rows, cols = tile_of(me[g])
        return to(g, ahead(g, n), o[g].at[pl.ds(5 * ahead(g, n), 5)], u[g].at[st, :, rows, cols], bck_s.at[g, n], bck_r.at[g, st, n])

    def bck_own(g, st):
        rows, cols = tile_of(me[g])
        return pltpu.make_async_copy(o[g].at[pl.ds(5 * me[g], 5)], u[g].at[st, :, rows, cols], local.at[g, 1])

    def fwd_start(g, st):
        loop(1, G, lambda n: fwd(g, st, n).start())
        fwd_own(g, st).start()

    def fwd_finish(g, st):
        fwd_own(g, st).wait()
        loop(1, G, lambda n: fwd(g, st, n).wait_recv())

    def bck_start(g, st):
        loop(1, G, lambda n: bck(g, st, n).start())
        bck_own(g, st).start()

    def bck_finish(g, st):
        bck_own(g, st).wait()
        loop(1, G, lambda n: bck(g, st, n).wait_recv())

    turn[...] = jnp.zeros((128, 128), F32)
    turn[0:N, 0:N] = h_in[...]
    hh, hl = split(h_in[...])
    gh, gl = split(-jnp.transpose(turn[...])[0:N, 0:N])

    def mix(g, st):
        left = (hh, hl) if g == 0 else (gh, gl)
        src = r[g].at[st].reshape(N * 16, 128)
        dst = o[g].reshape(N * 16, 128)
        for w in range(0, 16, 2):
            x = jnp.concatenate([src[pl.ds(w + e, N, stride=16), :] for e in range(2)], axis=1)
            x = dot3(*left, *split(x))
            for e in range(2):
                dst[pl.ds(w + e, N, stride=16), :] = x[:, 128 * e:128 * (e + 1)]

    def rsa(g, st):
        other = pl.multiple_of(HALF * (1 - lax.rem(me[g], 2)), 8)
        return to(g, partner[g], yp[g].at[pl.ds(other, HALF)], pa[g].at[st], rsa_s.at[g], rsa_r.at[g, st])

    def rsb(g, st, n):
        rows, cols = half_piece(ahead(g, 2 * n) // 2)
        return to(g, ahead(g, 2 * n), hb[g].at[rows, cols], pb[g].at[st, n], rsb_s.at[g, n], rsb_r.at[g, st, n])

    def ag(g, st, n):
        block = yf[g].at[st, *piece(me[g])]
        return to(g, ahead(g, 2 * n), block, block, ag_s.at[g, n], ag_r.at[g, st, n])

    def ag_own(g, st):
        block = yf[g].at[st, *piece(me[g])]
        return to(g, partner[g], block, block, ag_s.at[g, 8], ag_r.at[g, st, 8])

    def ag_sent(g, st, n):
        block = yf[g].at[st, *piece(behind(g, 2 * n))]
        return to(g, ahead(g, 2 * n), block, block, ag_s.at[g, n], ag_r.at[g, st, n])

    def ag_relay(g, st, n):
        block = yf[g].at[st, *piece(behind(g, 2 * n))]
        return to(g, partner[g], block, block, ag_s.at[g, 8 + n], ag_r.at[g, st, 8 + n])

    def rsa_finish(g, st):
        rsa(g, st).wait_recv()
        keep = pl.multiple_of(HALF * lax.rem(me[g], 2), 8)
        hb[g][...] = yp[g][pl.ds(keep, HALF), :] + pa[g][st]

    def rsb_start(st):
        rsa_finish(0, st)
        loop(1, 8, lambda n: rsb(0, st, n).start())

    beside = me[1] + 2 - 4 * lax.rem(me[1] // 2, 2)
    low = lax.rem(me[1] // 2, 2)

    def block_of(member):
        return (
            pl.ds(pl.multiple_of(HALF * lax.rem(member, 2), 8), HALF),
            pl.ds(pl.multiple_of(128 * (member // 4), 128), 128),
        )

    def col_x(st, n):
        cols = pl.ds(pl.multiple_of(128 * (ahead(1, 4 * n) // 4), 128), 128)
        return to(1, ahead(1, 4 * n), hb_c.at[:, cols], px.at[st, n], rsb_s.at[1, n], rsb_r.at[1, st, n])

    def col_y(st):
        rows = pl.ds(pl.multiple_of(PART * (1 - low), 8), PART)
        return to(1, beside, sx.at[rows], py.at[st], rsb_s.at[1, 4], rsb_r.at[1, st, 4])

    def col_gather_y(st, member):
        block = yf_c.at[st, *piece(member)]
        return to(1, beside, block, block, ag_s.at[1, 4], ag_r.at[1, st, 4])

    def col_gather_x(st, n, member):
        block = yf_c.at[st, *block_of(member)]
        return to(1, ahead(1, 4 * n), block, block, ag_s.at[1, n], ag_r.at[1, st, n])

    def col_gather_core(st, n):
        block = yf_c.at[st, *block_of(behind(1, 4 * n))]
        return to(1, partner[1], block, block, ag_s.at[1, 8 + n], ag_r.at[1, st, 8 + n])

    def col_1(st):
        rsa_finish(1, st)
        loop(1, 4, lambda n: col_x(st, n).start())

    def col_2(st):
        loop(1, 4, lambda n: col_x(st, n).wait_recv())
        cols = pl.ds(pl.multiple_of(128 * (me[1] // 4), 128), 128)
        sx[...] = (hb_c[:, cols] + px[st, 1]) + (px[st, 2] + px[st, 3])
        col_y(st).start()

    def col_3(st):
        col_y(st).wait_recv()
        rows, cols = piece(me[1])
        total = sx[pl.ds(pl.multiple_of(PART * low, 8), PART), :] + py[st]
        yf_c[st, rows, cols] = total * v_ref[0:1, cols]
        col_gather_y(st, me[1]).start()

    def col_4(st):
        col_gather_y(st, beside).wait_recv()
        loop(1, 4, lambda n: col_gather_x(st, n, me[1]).start())
        col_gather_core(st, 0).start()

    def col_5(st):
        def relay(n):
            col_gather_x(st, n, behind(1, 4 * n)).wait_recv()
            col_gather_core(st, n).start()
        loop(1, 4, relay)

    def col_6(st):
        loop(0, 4, lambda n: col_gather_core(st, n).wait_recv())

    def col_sent(st):
        rsa(1, st).wait_send()
        loop(1, 4, lambda n: col_x(st, n).wait_send())
        col_y(st).wait_send()
        col_gather_y(st, me[1]).wait_send()
        loop(1, 4, lambda n: col_gather_x(st, n, me[1]).wait_send())
        loop(0, 4, lambda n: col_gather_core(st, n).wait_send())

    def ag_start(g, st):
        loop(1, 8, lambda n: rsb(g, st, n).wait_recv())
        rows, cols = half_piece(me[g] // 2)
        total = hb[g][rows, cols]
        for n in range(1, 8):
            total = total + pb[g][st, n]
        rows, cols = piece(me[g])
        yf[g][st, rows, cols] = total * v_ref[0:1, cols]
        loop(1, 8, lambda n: ag(g, st, n).start())
        ag_own(g, st).start()

    def relay_start(g, st):
        def relay(n):
            ag_sent(g, st, n).wait_recv()
            ag_relay(g, st, n).start()
        loop(1, 8, relay)

    def ag_finish(g, st):
        ag_own(g, st).wait_recv()
        loop(1, 8, lambda n: ag_relay(g, st, n).wait_recv())

    for p in range(B):
        for t in range(4):
            aux_in[p * 20 + t * B:p * 20 + t * B + B, :] = aux_ref[p, :, 128 * t:128 * t + 128]
    aux_in[100:PART, :] = jnp.zeros((PART - 100, 128), F32)
    enter()
    aux_start(1)
    aux_start(0)
    zeros = jnp.zeros((512 - NB, 512), F32)
    wide[NB:512, :] = zeros
    start[:, 384:512] = jnp.zeros((NB, 128), F32)
    for k in range(B):
        for i in range(B):
            start[k * N:k * N + N, i * N:i * N + N] = x_in[i * N:i * N + N, k * N:k * N + N]
    pack(start, s_c)
    fwd_start(1, 0)
    wide[0:NB, :] = start[...]
    stage_b[...] = jnp.transpose(wide[...])
    pack(stage_b, s_r)
    fwd_start(0, 0)
    th[...], tl[...] = split(stage_b[0:NB, :])
    xh[...], xl[...] = split(start[...])
    stage_b[NB:512, :] = zeros
    y2h[NB:512, :] = zeros.astype(BF16)
    y2l[NB:512, :] = zeros.astype(BF16)
    for g in range(2):
        yp[g][NB:2 * HALF, :] = zeros[0:2 * HALF - NB]
    v_ref[...] = jnp.broadcast_to(v_in[...].reshape(1, NAUX), (8, NAUX))
    bdh[...] = jnp.zeros((512, 512), BF16)
    bdl[...] = jnp.zeros((512, 512), BF16)
    for i in range(B):
        bdh[i * N:i * N + N, i * N:i * N + N] = hh
        bdl[i * N:i * N + N, i * N:i * N + N] = hl

    def gather_left():
        aux_finish(1)
        for c in range(G):
            for i in range(B):
                for t in range(4):
                    stage_b[i * N + 5 * c:i * N + 5 * c + 5, 128 * t:128 * t + 128] = a_c[c, i * 20 + t * 5:i * 20 + t * 5 + 5, :]
        blh[...], bll[...] = split(stage_b[...])

    def gather_right():
        aux_finish(0)
        for c in range(G):
            for k in range(B):
                for t in range(4):
                    stage_b[k * N + 5 * c:k * N + 5 * c + 5, 128 * t:128 * t + 128] = a_r[c, pl.ds(t * 5 + k, 5, stride=20), :]
        brh[...], brl[...] = split(stage_b[...])

    def section(st, carry):
        @pl.when(st == 0)
        def _():
            gather_left()

        yp_r[0:NB, :] = dot3(xh[...], xl[...], blh[...], bll[...])
        rsa(0, st).start()

        @pl.when(st == 1)
        def _():
            fwd_start(0, st)
            fwd_start(1, st)

        @pl.when(st == 0)
        def _():
            gather_right()

        yp_c[0:NB, :] = dot3(th[...], tl[...], brh[...], brl[...])
        rsa(1, st).start()
        dloc[...] = local_terms()
        col_1(st)
        rsb_start(st)
        col_2(st)
        fwd_finish(1, st)
        mix(1, st)
        col_3(st)
        bck_start(1, st)
        fwd_finish(0, st)
        mix(0, st)
        col_4(st)
        ag_start(0, st)
        bck_start(0, st)
        col_5(st)
        relay_start(0, st)
        bck_finish(1, st)
        unpack(u_c.at[st], wide)
        f = dloc[...] + wide[0:NB, :]
        bck_finish(0, st)
        unpack(u_r.at[st], wide)
        dloc[...] = f + jnp.transpose(wide[...])[0:NB, :]
        col_6(st)
        y2h[0:NB, :], y2l[0:NB, :] = split(yf_c[st, 0:NB, :])
        dloc[...] = dloc[...] - dot3(brh[0:NB, :], brl[0:NB, :], y2h[...], y2l[...], NT)
        ag_finish(0, st)
        f = dloc[...] + dot3(*split(yf_r[st, 0:NB, :]), blh[...], bll[...], NT)

        for g in range(2):
            loop(1, G, lambda n: fwd(g, st, n).wait_send())
            loop(1, G, lambda n: bck(g, st, n).wait_send())
        rsa(0, st).wait_send()
        loop(1, 8, lambda n: rsb(0, st, n).wait_send())
        loop(1, 8, lambda n: ag(0, st, n).wait_send())
        ag_own(0, st).wait_send()
        loop(1, 8, lambda n: ag_relay(0, st, n).wait_send())
        col_sent(st)

        @pl.when(st == 0)
        def _():
            fsum[...] = f
            x = start[...] + time_step * f
            xa[...] = x
            wide[0:NB, :] = x
            xh[...], xl[...] = split(x)
            xa_t = jnp.transpose(wide[...])[0:NB, :]
            stage_b[0:NB, :] = xa_t
            th[...], tl[...] = split(xa_t)
            pack(stage_b, s_r)
            pack(xa, s_c)
            for g in range(2):
                aux_sent(g)

        @pl.when(st == 1)
        def _():
            xa[...] = start[...] + time_step / 2.0 * (fsum[...] + f)
            for k in range(B):
                for i in range(B):
                    out_ref[i * N:i * N + N, k * N:k * N + N] = xa[k * N:k * N + N, i * N:i * N + N]

        return carry

    def local_terms():
        left = dot3(bdh[0:NB, 0:512], bdl[0:NB, 0:512], *pad_rows())
        return left - dot3(xh[...], xl[...], bdh[...], bdl[...])

    def pad_rows():
        z = jnp.zeros((512 - NB, 512), BF16)
        return jnp.concatenate([xh[...], z], axis=0), jnp.concatenate([xl[...], z], axis=0)

    lax.fori_loop(0, 2, section, 0)


def shards(pairs, one_body, aux, weights):
    vmem = pl.BlockSpec(memory_space=pltpu.VMEM)
    f32 = lambda *shape: pltpu.VMEM(shape, F32)
    b16 = lambda *shape: pltpu.VMEM(shape, BF16)
    dma = lambda *shape: pltpu.SemaphoreType.DMA(shape)
    return pl.pallas_call(
        kernel,
        out_shape=jax.ShapeDtypeStruct((NB, NB), F32),
        in_specs=[vmem] * 4,
        out_specs=vmem,
        scratch_shapes=[
            f32(NB, 512), f32(PART, 128), f32(8, NAUX), f32(128, 128),
            f32(NB, 512), b16(NB, 512), b16(NB, 512), b16(NB, 512), b16(NB, 512),
            f32(512, 512), f32(512, 512), f32(NB, 512), f32(NB, 512),
            *[b16(512, 512)] * 8,
            *[f32(B, N, 512)] * 2, *[f32(2, N, 16, 128)] * 2, *[f32(N, 16, 128)] * 2, *[f32(2, B, N, 512)] * 2,
            *[f32(G, PART, 128)] * 2, *[f32(2 * HALF, 512)] * 2, *[f32(2, HALF, 512)] * 2, *[f32(HALF, 512)] * 2,
            f32(2, 8, PART, 128), f32(2, 4, HALF, 128), f32(2, PART, 128), f32(HALF, 128), *[f32(2, 2 * HALF, 512)] * 2,
            dma(2, 2), dma(2, 16), dma(2, 16), dma(2, 16), dma(2, 2, 16), dma(2, 16), dma(2, 2, 16),
            dma(2), dma(2, 2), dma(2, 8), dma(2, 2, 8), dma(2, 16), dma(2, 2, 16),
        ],
        compiler_params=pltpu.CompilerParams(collective_id=0, has_side_effects=True, vmem_limit_bytes=60 * 1024 * 1024),
        name="heun",
    )(pairs, aux, weights, one_body)


def solution(mesh):
    in_specs = (P("row", "col"), P(), P("row", "col", None), P())
    out_specs = P("row", "col")
    return jax.shard_map(shards, mesh=mesh, in_specs=in_specs, out_specs=out_specs, check_vma=False)
```

```python
import functools

import jax
import jax.numpy as jnp
from jax import lax
from jax.experimental import pallas as pl
from jax.experimental.pallas import tpu as pltpu
from jax.sharding import PartitionSpec as P

time_step = 0.15
MESH = pl.DeviceIdType.MESH
F32, BF16 = jnp.float32, jnp.bfloat16
N, G, B, NAUX = 80, 16, 5, 512
NB = N * B
HALF, PART = 208, 104
NN = (((1,), (0,)), ((), ()))
NT = (((1,), (1,)), ((), ()))


def split(x):
    high = x.astype(BF16)
    return high, (x - high.astype(F32)).astype(BF16)


def dot3(ah, al, bh, bl, dims=NN):
    dot = functools.partial(lax.dot_general, dimension_numbers=dims, preferred_element_type=F32)
    return dot(ah, bh) + (dot(ah, bl) + dot(al, bh))


def tile_of(part):
    return pl.ds(pl.multiple_of(16 * lax.rem(part, 5), 16), 16), pl.ds(pl.multiple_of(128 * (part // 5), 128), 128)


def half_piece(z):
    return pl.ds(pl.multiple_of(PART * lax.rem(z, 2), 8), PART), pl.ds(pl.multiple_of(128 * (z // 2), 128), 128)


def piece(member):
    z = member // 2
    return (
        pl.ds(pl.multiple_of(HALF * lax.rem(member, 2) + PART * lax.rem(z, 2), 8), PART),
        pl.ds(pl.multiple_of(128 * (z // 2), 128), 128),
    )


def pack(x_ref, s_ref):
    for i in range(B):
        s_ref[i, :, 0:384] = x_ref[i * N:(i + 1) * N, 0:384]
        for lo, hi in ((0, 8), (8, 10)):
            tail = x_ref[i * N + 8 * lo:i * N + 8 * lo + 8, 384:512]
            for m in range(lo + 1, hi):
                tail = tail + pltpu.roll(x_ref[i * N + 8 * m:i * N + 8 * m + 8, 384:512], 16 * (m - lo), 1)
            s_ref[i, lo:lo + 8, 384:512] = tail


def unpack(u_ref, x_ref):
    lane = lax.broadcasted_iota(jnp.int32, (8, 128), 1)
    for i in range(B):
        x_ref[i * N:(i + 1) * N, 0:384] = u_ref[i, :, 0:384]
        for m in range(10):
            lo = 8 * (m // 8)
            tail = u_ref[i, lo:lo + 8, 384:512]
            if m % 8:
                tail = pltpu.roll(tail, 128 - 16 * (m % 8), 1)
            x_ref[i * N + 8 * m:i * N + 8 * m + 8, 384:512] = jnp.where(lane < 16, tail, 0.0)


def kernel(
    x_in, aux_ref, v_in, h_in, out_ref,
    start, aux_in, v_ref, turn,
    xa, xh, xl, th, tl, wide, stage_b, dloc, fsum,
    blh, bll, brh, brl, bdh, bdl, y2h, y2l,
    s_r, s_c, r_r, r_c, o_r, o_c, u_r, u_c,
    a_r, a_c, yp_r, yp_c, pa_r, pa_c, hb_r, hb_c, pb_r, px, py, sx, yf_r, yf_c,
    local, aux_s, aux_r, fwd_s, fwd_r, bck_s, bck_r, rsa_s, rsa_r, rst_s, rst_r, rsb_s, rsb_r, ag_s, ag_r,
):
    me = (lax.axis_index("row"), lax.axis_index("col"))
    s, r, o, u = (s_r, s_c), (r_r, r_c), (o_r, o_c), (u_r, u_c)
    a, yp, pa, hb, pb, yf = (a_r, a_c), (yp_r, yp_c), (pa_r, pa_c), (hb_r, hb_c), (pb_r, None), (yf_r, yf_c)
    partner = tuple(m + 1 - 2 * lax.rem(m, 2) for m in me)

    def at(g, member):
        return (member, me[1]) if g == 0 else (me[0], member)

    def to(g, member, src, dst, ssem, rsem):
        return pltpu.make_async_remote_copy(
            src_ref=src, dst_ref=dst, send_sem=ssem, recv_sem=rsem, device_id=at(g, member), device_id_type=MESH
        )

    def ahead(g, n):
        return lax.rem(me[g] + n, G)

    def behind(g, n):
        return lax.rem(me[g] + G - n, G)

    def loop(lo, hi, body):
        def step(n, carry):
            body(n)
            return carry
        lax.fori_loop(lo, hi, step, 0)

    def enter():
        barrier = pltpu.get_barrier_semaphore()
        for g in range(2):
            loop(1, G, lambda n: pl.semaphore_signal(barrier, inc=1, device_id=at(g, ahead(g, n)), device_id_type=MESH))
        pl.semaphore_wait(barrier, 2 * (G - 1))

    def aux_copy(g, n):
        return to(g, ahead(g, 2 * n), aux_in, a[g].at[me[g]], aux_s.at[g, n], aux_r.at[g, n])

    def aux_relay(g, n):
        src = behind(g, 2 * n)
        block = a[g].at[src]
        return to(g, partner[g], block, block, aux_s.at[g, 8 + n], aux_r.at[g, 8 + n])

    def aux_own(g):
        return to(g, partner[g], aux_in, a[g].at[me[g]], aux_s.at[g, 8], aux_r.at[g, 8])

    def aux_start(g):
        loop(1, 8, lambda n: aux_copy(g, n).start())
        aux_own(g).start()

    def aux_relays(g):
        def relay(n):
            aux_copy(g, n).wait_recv()
            aux_relay(g, n).start()
        loop(1, 8, relay)

    def aux_finish(g):
        a[g][me[g]] = aux_in[...]
        aux_own(g).wait_recv()
        loop(1, 8, lambda n: aux_relay(g, n).wait_recv())

    def aux_sent(g):
        loop(1, 8, lambda n: aux_copy(g, n).wait_send())
        loop(1, 8, lambda n: aux_relay(g, n).wait_send())
        aux_own(g).wait_send()

    beside = me[1] + 2 - 4 * lax.rem(me[1] // 2, 2)
    low = lax.rem(me[1] // 2, 2)

    def beside_of(member):
        return member + 2 - 4 * lax.rem(member // 2, 2)

    def left_y(member):
        return to(1, beside, aux_in, a_c.at[member], aux_s.at[1, 0], aux_r.at[1, 0])

    def left_x(n, member):
        return to(1, ahead(1, 4 * n), aux_in, a_c.at[member], aux_s.at[1, n], aux_r.at[1, n])

    def left_x2(n, member):
        block = a_c.at[member]
        return to(1, ahead(1, 4 * n), block, block, aux_s.at[1, 4 + n], aux_r.at[1, 4 + n])

    def left_core(n, member):
        block = a_c.at[member]
        return to(1, partner[1], block, block, aux_s.at[1, 8 + n], aux_r.at[1, 8 + n])

    def left_own():
        return to(1, partner[1], aux_in, a_c.at[me[1]], aux_s.at[1, 8], aux_r.at[1, 8])

    def left_start():
        left_y(me[1]).start()
        loop(1, 4, lambda n: left_x(n, me[1]).start())
        left_own().start()

    def left_finish():
        a_c[me[1]] = aux_in[...]
        left_y(beside).wait_recv()
        loop(1, 4, lambda n: left_x2(n, beside).start())
        left_core(4, beside).start()

        def relay(n):
            src = behind(1, 4 * n)
            left_x(n, src).wait_recv()
            left_core(n, src).start()
        loop(1, 4, relay)

        def relay2(n):
            src = beside_of(behind(1, 4 * n))
            left_x2(n, src).wait_recv()
            left_core(4 + n, src).start()
        loop(1, 4, relay2)
        loop(0, 8, lambda n: left_core(n, me[1]).wait_recv())

    def left_sent():
        left_y(me[1]).wait_send()
        loop(1, 4, lambda n: left_x(n, me[1]).wait_send())
        loop(1, 4, lambda n: left_x2(n, beside).wait_send())
        loop(0, 8, lambda n: left_core(n, me[1]).wait_send())

    def fwd(g, st, n):
        rows, cols = tile_of(ahead(g, n))
        return to(g, ahead(g, n), s[g].at[:, rows, cols], r[g].at[st, pl.ds(5 * me[g], 5)], fwd_s.at[g, n], fwd_r.at[g, st, n])

    def fwd_own(g, st):
        rows, cols = tile_of(me[g])
        return pltpu.make_async_copy(s[g].at[:, rows, cols], r[g].at[st, pl.ds(5 * me[g], 5)], local.at[g, 0])

    def bck(g, st, n):
        rows, cols = tile_of(me[g])
        return to(g, ahead(g, n), o[g].at[pl.ds(5 * ahead(g, n), 5)], u[g].at[st, :, rows, cols], bck_s.at[g, n], bck_r.at[g, st, n])

    def bck_own(g, st):
        rows, cols = tile_of(me[g])
        return pltpu.make_async_copy(o[g].at[pl.ds(5 * me[g], 5)], u[g].at[st, :, rows, cols], local.at[g, 1])

    def fwd_start(g, st):
        loop(1, G, lambda n: fwd(g, st, n).start())
        fwd_own(g, st).start()

    def fwd_finish(g, st):
        fwd_own(g, st).wait()
        loop(1, G, lambda n: fwd(g, st, n).wait_recv())

    def bck_start(g, st):
        loop(1, G, lambda n: bck(g, st, n).start())
        bck_own(g, st).start()

    def bck_finish(g, st):
        bck_own(g, st).wait()
        loop(1, G, lambda n: bck(g, st, n).wait_recv())

    turn[...] = jnp.zeros((128, 128), F32)
    turn[0:N, 0:N] = h_in[...]
    hh, hl = split(h_in[...])
    gh, gl = split(-jnp.transpose(turn[...])[0:N, 0:N])

    def mix(g, st):
        left = (hh, hl) if g == 0 else (gh, gl)
        src = r[g].at[st].reshape(N * 16, 128)
        dst = o[g].reshape(N * 16, 128)
        for w in range(0, 16, 2):
            x = jnp.concatenate([src[pl.ds(w + e, N, stride=16), :] for e in range(2)], axis=1)
            x = dot3(*left, *split(x))
            for e in range(2):
                dst[pl.ds(w + e, N, stride=16), :] = x[:, 128 * e:128 * (e + 1)]

    def rsa(g, st):
        other = pl.multiple_of(HALF * (1 - lax.rem(me[g], 2)), 8)
        return to(g, partner[g], yp[g].at[pl.ds(other, HALF)], pa[g].at[st], rsa_s.at[g], rsa_r.at[g, st])

    def rsb(g, st, n):
        rows, cols = half_piece(ahead(g, 2 * n) // 2)
        return to(g, ahead(g, 2 * n), hb[g].at[rows, cols], pb[g].at[st, n], rsb_s.at[g, n], rsb_r.at[g, st, n])

    def ag(g, st, n):
        block = yf[g].at[st, *piece(me[g])]
        return to(g, ahead(g, 2 * n), block, block, ag_s.at[g, n], ag_r.at[g, st, n])

    def ag_own(g, st):
        block = yf[g].at[st, *piece(me[g])]
        return to(g, partner[g], block, block, ag_s.at[g, 8], ag_r.at[g, st, 8])

    def ag_sent(g, st, n):
        block = yf[g].at[st, *piece(behind(g, 2 * n))]
        return to(g, ahead(g, 2 * n), block, block, ag_s.at[g, n], ag_r.at[g, st, n])

    def ag_relay(g, st, n):
        block = yf[g].at[st, *piece(behind(g, 2 * n))]
        return to(g, partner[g], block, block, ag_s.at[g, 8 + n], ag_r.at[g, st, 8 + n])

    def rsa_finish(g, st):
        rsa(g, st).wait_recv()
        keep = pl.multiple_of(HALF * lax.rem(me[g], 2), 8)
        hb[g][...] = yp[g][pl.ds(keep, HALF), :] + pa[g][st]

    zi = me[0] // 2

    def rsa_tile(st, t):
        other = pl.multiple_of(HALF * (1 - lax.rem(me[0], 2)), 8)
        cols = pl.ds(pl.multiple_of(128 * t, 128), 128)
        return to(0, partner[0], yp_r.at[pl.ds(other, HALF), cols], pa_r.at[st, :, cols], rst_s.at[t], rst_r.at[st, t])

    def turn_of(t):
        return lax.rem(zi // 2 + 1 + t, 4)

    def rsa_start(st):
        loop(0, 4, lambda t: rsa_tile(st, turn_of(t)).start())

    def rsb_start(st):
        keep = pl.multiple_of(HALF * lax.rem(me[0], 2), 8)

        def tile(t):
            t = turn_of(t)
            rsa_tile(st, t).wait_recv()
            cols = pl.ds(pl.multiple_of(128 * t, 128), 128)
            hb_r[:, cols] = yp_r[pl.ds(keep, HALF), cols] + pa_r[st, :, cols]
            for e in range(2):
                n = lax.rem(2 * t + e - zi + 8, 8)

                @pl.when(n != 0)
                def _():
                    rsb(0, st, n).start()
        loop(0, 4, tile)

    def block_of(member):
        return (
            pl.ds(pl.multiple_of(HALF * lax.rem(member, 2), 8), HALF),
            pl.ds(pl.multiple_of(128 * (member // 4), 128), 128),
        )

    def col_x(st, n):
        cols = pl.ds(pl.multiple_of(128 * (ahead(1, 4 * n) // 4), 128), 128)
        return to(1, ahead(1, 4 * n), hb_c.at[:, cols], px.at[st, n], rsb_s.at[1, n], rsb_r.at[1, st, n])

    def col_y(st):
        rows = pl.ds(pl.multiple_of(PART * (1 - low), 8), PART)
        return to(1, beside, sx.at[rows], py.at[st], rsb_s.at[1, 4], rsb_r.at[1, st, 4])

    def col_gather_y(st, member):
        block = yf_c.at[st, *piece(member)]
        return to(1, beside, block, block, ag_s.at[1, 4], ag_r.at[1, st, 4])

    def col_gather_x(st, n, member):
        block = yf_c.at[st, *block_of(member)]
        return to(1, ahead(1, 4 * n), block, block, ag_s.at[1, n], ag_r.at[1, st, n])

    def col_gather_core(st, n):
        block = yf_c.at[st, *block_of(behind(1, 4 * n))]
        return to(1, partner[1], block, block, ag_s.at[1, 8 + n], ag_r.at[1, st, 8 + n])

    def col_1(st):
        rsa_finish(1, st)
        loop(1, 4, lambda n: col_x(st, n).start())

    def col_2(st):
        loop(1, 4, lambda n: col_x(st, n).wait_recv())
        cols = pl.ds(pl.multiple_of(128 * (me[1] // 4), 128), 128)
        sx[...] = (hb_c[:, cols] + px[st, 1]) + (px[st, 2] + px[st, 3])
        col_y(st).start()

    def col_3(st):
        col_y(st).wait_recv()
        rows, cols = piece(me[1])
        total = sx[pl.ds(pl.multiple_of(PART * low, 8), PART), :] + py[st]
        yf_c[st, rows, cols] = total * v_ref[0:1, cols]
        col_gather_y(st, me[1]).start()

    def col_4(st):
        col_gather_y(st, beside).wait_recv()
        loop(1, 4, lambda n: col_gather_x(st, n, me[1]).start())
        col_gather_core(st, 0).start()

    def col_5(st):
        def relay(n):
            col_gather_x(st, n, behind(1, 4 * n)).wait_recv()
            col_gather_core(st, n).start()
        loop(1, 4, relay)

    def col_6(st):
        loop(0, 4, lambda n: col_gather_core(st, n).wait_recv())

    def col_sent(st):
        rsa(1, st).wait_send()
        loop(1, 4, lambda n: col_x(st, n).wait_send())
        col_y(st).wait_send()
        col_gather_y(st, me[1]).wait_send()
        loop(1, 4, lambda n: col_gather_x(st, n, me[1]).wait_send())
        loop(0, 4, lambda n: col_gather_core(st, n).wait_send())

    def ag_start(g, st):
        loop(1, 8, lambda n: rsb(g, st, n).wait_recv())
        rows, cols = half_piece(me[g] // 2)
        total = hb[g][rows, cols]
        for n in range(1, 8):
            total = total + pb[g][st, n]
        rows, cols = piece(me[g])
        yf[g][st, rows, cols] = total * v_ref[0:1, cols]
        loop(1, 8, lambda n: ag(g, st, n).start())
        ag_own(g, st).start()

    def relay_start(g, st):
        def relay(n):
            ag_sent(g, st, n).wait_recv()
            ag_relay(g, st, n).start()
        loop(1, 8, relay)

    def ag_finish(g, st):
        ag_own(g, st).wait_recv()
        loop(1, 8, lambda n: ag_relay(g, st, n).wait_recv())

    for p in range(B):
        for t in range(4):
            aux_in[p * 20 + t * B:p * 20 + t * B + B, :] = aux_ref[p, :, 128 * t:128 * t + 128]
    aux_in[100:PART, :] = jnp.zeros((PART - 100, 128), F32)
    enter()
    left_start()
    aux_start(0)
    zeros = jnp.zeros((512 - NB, 512), F32)
    wide[NB:512, :] = zeros
    start[:, 384:512] = jnp.zeros((NB, 128), F32)
    for k in range(B):
        for i in range(B):
            start[k * N:k * N + N, i * N:i * N + N] = x_in[i * N:i * N + N, k * N:k * N + N]
    pack(start, s_c)
    wide[0:NB, :] = start[...]
    stage_b[...] = jnp.transpose(wide[...])
    pack(stage_b, s_r)
    fwd_start(0, 0)
    th[...], tl[...] = split(stage_b[0:NB, :])
    xh[...], xl[...] = split(start[...])
    stage_b[NB:512, :] = zeros
    y2h[NB:512, :] = zeros.astype(BF16)
    y2l[NB:512, :] = zeros.astype(BF16)
    for g in range(2):
        yp[g][NB:2 * HALF, :] = zeros[0:2 * HALF - NB]
    v_ref[...] = jnp.broadcast_to(v_in[...].reshape(1, NAUX), (8, NAUX))
    bdh[...] = jnp.zeros((512, 512), BF16)
    bdl[...] = jnp.zeros((512, 512), BF16)
    for i in range(B):
        bdh[i * N:i * N + N, i * N:i * N + N] = hh
        bdl[i * N:i * N + N, i * N:i * N + N] = hl

    def gather_left():
        left_finish()
        for c in range(G):
            for i in range(B):
                for t in range(4):
                    stage_b[i * N + 5 * c:i * N + 5 * c + 5, 128 * t:128 * t + 128] = a_c[c, i * 20 + t * 5:i * 20 + t * 5 + 5, :]
        blh[...], bll[...] = split(stage_b[...])

    def gather_right():
        aux_finish(0)
        for c in range(G):
            for k in range(B):
                for t in range(4):
                    stage_b[k * N + 5 * c:k * N + 5 * c + 5, 128 * t:128 * t + 128] = a_r[c, pl.ds(t * 5 + k, 5, stride=20), :]
        brh[...], brl[...] = split(stage_b[...])

    def section(st):
        if st == 0:
            gather_left()
        if st == 0:
            yp_r[0:NB, :] = dot3(xh[...], xl[...], blh[...], bll[...])
            rsa_start(st)
            aux_relays(0)
            fwd_start(1, st)
            dloc[...] = local_terms()
            rsb_start(st)
            gather_right()
            yp_c[0:NB, :] = dot3(th[...], tl[...], brh[...], brl[...])
            rsa(1, st).start()
            col_1(st)
            fwd_finish(0, st)
            mix(0, st)
            bck_start(0, st)
            col_2(st)
            col_3(st)
            fwd_finish(1, st)
            mix(1, st)
            ag_start(0, st)
            col_4(st)
            bck_start(1, st)
        else:
            yp_c[0:NB, :] = dot3(th[...], tl[...], brh[...], brl[...])
            rsa(1, st).start()
            dloc[...] = local_terms()
            col_1(st)
            rsb_start(st)
            col_2(st)
            fwd_finish(1, st)
            mix(1, st)
            col_3(st)
            bck_start(1, st)
            fwd_finish(0, st)
            mix(0, st)
            col_4(st)
            ag_start(0, st)
            bck_start(0, st)
        col_5(st)
        relay_start(0, st)
        bck_finish(1, st)
        unpack(u_c.at[st], wide)
        dloc[...] = dloc[...] + wide[0:NB, :]

        def row_term():
            bck_finish(0, st)
            unpack(u_r.at[st], wide)
            return dloc[...] + jnp.transpose(wide[...])[0:NB, :]

        if st == 0:
            dloc[...] = row_term()
        col_6(st)
        y2h[0:NB, :], y2l[0:NB, :] = split(yf_c[st, 0:NB, :])
        dloc[...] = dloc[...] - dot3(brh[0:NB, :], brl[0:NB, :], y2h[...], y2l[...], NT)
        ag_finish(0, st)
        f = dot3(*split(yf_r[st, 0:NB, :]), blh[...], bll[...], NT)
        if st == 0:
            f = dloc[...] + f
        else:
            dloc[...] = dloc[...] + f
            f = row_term()

        def sent():
            for g in range(2):
                loop(1, G, lambda n: bck(g, st, n).wait_send())
            loop(1, 8, lambda n: rsb(0, st, n).wait_send())
            loop(1, 8, lambda n: ag(0, st, n).wait_send())
            ag_own(0, st).wait_send()
            loop(1, 8, lambda n: ag_relay(0, st, n).wait_send())
            col_sent(st)

        def first_sent():
            for g in range(2):
                loop(1, G, lambda n: fwd(g, st, n).wait_send())
            loop(0, 4, lambda t: rsa_tile(st, t).wait_send())

        if st == 0:
            fsum[...] = f
            x = start[...] + time_step * f
            xa[...] = x
            wide[0:NB, :] = x
            xh[...], xl[...] = split(x)
            first_sent()
            yp_r[0:NB, :] = dot3(xh[...], xl[...], blh[...], bll[...])
            rsa_start(1)
            stage_b[0:NB, :] = jnp.transpose(wide[...])[0:NB, :]
            pack(stage_b, s_r)
            fwd_start(0, 1)
            pack(xa, s_c)
            fwd_start(1, 1)
            th[...], tl[...] = split(stage_b[0:NB, :])
            sent()
            left_sent()
            aux_sent(0)
        if st == 1:
            first_sent()
            sent()
            xa[...] = start[...] + time_step / 2.0 * (fsum[...] + f)
            for k in range(B):
                for i in range(B):
                    out_ref[i * N:i * N + N, k * N:k * N + N] = xa[k * N:k * N + N, i * N:i * N + N]

    def local_terms():
        left = dot3(bdh[0:NB, 0:512], bdl[0:NB, 0:512], *pad_rows())
        return left - dot3(xh[...], xl[...], bdh[...], bdl[...])

    def pad_rows():
        z = jnp.zeros((512 - NB, 512), BF16)
        return jnp.concatenate([xh[...], z], axis=0), jnp.concatenate([xl[...], z], axis=0)

    section(0)
    section(1)


def shards(pairs, one_body, aux, weights):
    vmem = pl.BlockSpec(memory_space=pltpu.VMEM)
    f32 = lambda *shape: pltpu.VMEM(shape, F32)
    b16 = lambda *shape: pltpu.VMEM(shape, BF16)
    dma = lambda *shape: pltpu.SemaphoreType.DMA(shape)
    return pl.pallas_call(
        kernel,
        out_shape=jax.ShapeDtypeStruct((NB, NB), F32),
        in_specs=[vmem] * 4,
        out_specs=vmem,
        scratch_shapes=[
            f32(NB, 512), f32(PART, 128), f32(8, NAUX), f32(128, 128),
            f32(NB, 512), b16(NB, 512), b16(NB, 512), b16(NB, 512), b16(NB, 512),
            f32(512, 512), f32(512, 512), f32(NB, 512), f32(NB, 512),
            *[b16(512, 512)] * 8,
            *[f32(B, N, 512)] * 2, *[f32(2, N, 16, 128)] * 2, *[f32(N, 16, 128)] * 2, *[f32(2, B, N, 512)] * 2,
            *[f32(G, PART, 128)] * 2, *[f32(2 * HALF, 512)] * 2, *[f32(2, HALF, 512)] * 2, *[f32(HALF, 512)] * 2,
            f32(2, 8, PART, 128), f32(2, 4, HALF, 128), f32(2, PART, 128), f32(HALF, 128), *[f32(2, 2 * HALF, 512)] * 2,
            dma(2, 2), dma(2, 16), dma(2, 16), dma(2, 16), dma(2, 2, 16), dma(2, 16), dma(2, 2, 16),
            dma(2), dma(2, 2), dma(4), dma(2, 4), dma(2, 8), dma(2, 2, 8), dma(2, 16), dma(2, 2, 16),
        ],
        compiler_params=pltpu.CompilerParams(collective_id=0, has_side_effects=True, vmem_limit_bytes=60 * 1024 * 1024),
        name="heun",
    )(pairs, aux, weights, one_body)


def solution(mesh):
    in_specs = (P("row", "col"), P(), P("row", "col", None), P())
    out_specs = P("row", "col")
    return jax.shard_map(shards, mesh=mesh, in_specs=in_specs, out_specs=out_specs, check_vma=False)
```

```python
import functools

import jax
import jax.numpy as jnp
from jax import lax
from jax.experimental import pallas as pl
from jax.experimental.pallas import tpu as pltpu
from jax.sharding import PartitionSpec as P

time_step = 0.15
MESH = pl.DeviceIdType.MESH
F32, BF16 = jnp.float32, jnp.bfloat16
N, G, B, NAUX = 80, 16, 5, 512
NB = N * B
HALF, PART = 208, 104
NN = (((1,), (0,)), ((), ()))
NT = (((1,), (1,)), ((), ()))


def split(x):
    high = x.astype(BF16)
    return high, (x - high.astype(F32)).astype(BF16)


def dot3(ah, al, bh, bl, dims=NN):
    dot = functools.partial(lax.dot_general, dimension_numbers=dims, preferred_element_type=F32)
    return dot(ah, bh) + (dot(ah, bl) + dot(al, bh))


def tile_of(part):
    return pl.ds(pl.multiple_of(16 * lax.rem(part, 5), 16), 16), pl.ds(pl.multiple_of(128 * (part // 5), 128), 128)


def half_piece(z):
    return pl.ds(pl.multiple_of(PART * lax.rem(z, 2), 8), PART), pl.ds(pl.multiple_of(128 * (z // 2), 128), 128)


def piece(member):
    z = member // 2
    return (
        pl.ds(pl.multiple_of(HALF * lax.rem(member, 2) + PART * lax.rem(z, 2), 8), PART),
        pl.ds(pl.multiple_of(128 * (z // 2), 128), 128),
    )


def pack(x_ref, s_ref):
    for i in range(B):
        s_ref[i, :, 0:384] = x_ref[i * N:(i + 1) * N, 0:384]
        for lo, hi in ((0, 8), (8, 10)):
            tail = x_ref[i * N + 8 * lo:i * N + 8 * lo + 8, 384:512]
            for m in range(lo + 1, hi):
                tail = tail + pltpu.roll(x_ref[i * N + 8 * m:i * N + 8 * m + 8, 384:512], 16 * (m - lo), 1)
            s_ref[i, lo:lo + 8, 384:512] = tail


def unpack(u_ref, x_ref):
    lane = lax.broadcasted_iota(jnp.int32, (8, 128), 1)
    for i in range(B):
        x_ref[i * N:(i + 1) * N, 0:384] = u_ref[i, :, 0:384]
        for m in range(10):
            lo = 8 * (m // 8)
            tail = u_ref[i, lo:lo + 8, 384:512]
            if m % 8:
                tail = pltpu.roll(tail, 128 - 16 * (m % 8), 1)
            x_ref[i * N + 8 * m:i * N + 8 * m + 8, 384:512] = jnp.where(lane < 16, tail, 0.0)


def kernel(
    x_in, aux_ref, v_in, h_in, out_ref,
    start, aux_in, v_ref, turn,
    xa, xh, xl, th, tl, wide, stage_b, dloc, fsum,
    blh, bll, brh, brl, bdh, bdl, y2h, y2l,
    s_r, s_c, r_r, r_c, o_r, o_c, u_r, u_c,
    d_in, d_c, dh, dl, yx, a_r, a_c, yp_r, yp_c, pa_r, pa_c, hb_r, hb_c, pb_r, px, py, sx, yf_r, yf_c,
    local, aux_s, aux_r, fwd_s, fwd_r, bck_s, bck_r, rsa_s, rsa_r, rst_s, rst_r, rsb_s, rsb_r, ag_s, ag_r,
):
    me = (lax.axis_index("row"), lax.axis_index("col"))
    s, r, o, u = (s_r, s_c), (r_r, r_c), (o_r, o_c), (u_r, u_c)
    a, yp, pa, hb, pb, yf = (a_r, a_c), (yp_r, yp_c), (pa_r, pa_c), (hb_r, hb_c), (pb_r, None), (yf_r, yf_c)
    partner = tuple(m + 1 - 2 * lax.rem(m, 2) for m in me)

    def at(g, member):
        return (member, me[1]) if g == 0 else (me[0], member)

    def to(g, member, src, dst, ssem, rsem):
        return pltpu.make_async_remote_copy(
            src_ref=src, dst_ref=dst, send_sem=ssem, recv_sem=rsem, device_id=at(g, member), device_id_type=MESH
        )

    def ahead(g, n):
        return lax.rem(me[g] + n, G)

    def behind(g, n):
        return lax.rem(me[g] + G - n, G)

    def loop(lo, hi, body):
        def step(n, carry):
            body(n)
            return carry
        lax.fori_loop(lo, hi, step, 0)

    def enter():
        barrier = pltpu.get_barrier_semaphore()
        for g in range(2):
            loop(1, G, lambda n: pl.semaphore_signal(barrier, inc=1, device_id=at(g, ahead(g, n)), device_id_type=MESH))
        pl.semaphore_wait(barrier, 2 * (G - 1))

    def aux_copy(g, n):
        return to(g, ahead(g, 2 * n), aux_in, a[g].at[me[g]], aux_s.at[g, n], aux_r.at[g, n])

    def aux_relay(g, n):
        src = behind(g, 2 * n)
        block = a[g].at[src]
        return to(g, partner[g], block, block, aux_s.at[g, 8 + n], aux_r.at[g, 8 + n])

    def aux_own(g):
        return to(g, partner[g], aux_in, a[g].at[me[g]], aux_s.at[g, 8], aux_r.at[g, 8])

    def aux_start(g):
        loop(1, 8, lambda n: aux_copy(g, n).start())
        aux_own(g).start()

    def aux_relays(g):
        def relay(n):
            aux_copy(g, n).wait_recv()
            aux_relay(g, n).start()
        loop(1, 8, relay)

    def aux_finish(g):
        a[g][me[g]] = aux_in[...]
        aux_own(g).wait_recv()
        loop(1, 8, lambda n: aux_relay(g, n).wait_recv())

    def aux_sent(g):
        loop(1, 8, lambda n: aux_copy(g, n).wait_send())
        loop(1, 8, lambda n: aux_relay(g, n).wait_send())
        aux_own(g).wait_send()

    beside = me[1] + 2 - 4 * lax.rem(me[1] // 2, 2)
    low = lax.rem(me[1] // 2, 2)

    own, gathered = (aux_in, d_in), (a_c, d_c)

    def beside_of(member):
        return member + 2 - 4 * lax.rem(member // 2, 2)

    def left_y(w, member):
        return to(1, beside, own[w], gathered[w].at[member], aux_s.at[1 + w, 0], aux_r.at[1 + w, 0])

    def left_x(w, n, member):
        return to(1, ahead(1, 4 * n), own[w], gathered[w].at[member], aux_s.at[1 + w, n], aux_r.at[1 + w, n])

    def left_x2(w, n, member):
        block = gathered[w].at[member]
        return to(1, ahead(1, 4 * n), block, block, aux_s.at[1 + w, 4 + n], aux_r.at[1 + w, 4 + n])

    def left_core(w, n, member):
        block = gathered[w].at[member]
        return to(1, partner[1], block, block, aux_s.at[1 + w, 8 + n], aux_r.at[1 + w, 8 + n])

    def left_own(w):
        return to(1, partner[1], own[w], gathered[w].at[me[1]], aux_s.at[1 + w, 8], aux_r.at[1 + w, 8])

    def left_start(w):
        left_y(w, me[1]).start()
        loop(1, 4, lambda n: left_x(w, n, me[1]).start())
        left_own(w).start()

    def left_finish(w):
        gathered[w][me[1]] = own[w][...]
        left_y(w, beside).wait_recv()
        loop(1, 4, lambda n: left_x2(w, n, beside).start())
        left_core(w, 4, beside).start()

        def relay(n):
            src = behind(1, 4 * n)
            left_x(w, n, src).wait_recv()
            left_core(w, n, src).start()
        loop(1, 4, relay)

        def relay2(n):
            src = beside_of(behind(1, 4 * n))
            left_x2(w, n, src).wait_recv()
            left_core(w, 4 + n, src).start()
        loop(1, 4, relay2)
        loop(0, 8, lambda n: left_core(w, n, me[1]).wait_recv())

    def left_sent(w):
        left_y(w, me[1]).wait_send()
        loop(1, 4, lambda n: left_x(w, n, me[1]).wait_send())
        loop(1, 4, lambda n: left_x2(w, n, beside).wait_send())
        loop(0, 8, lambda n: left_core(w, n, me[1]).wait_send())

    def fwd(g, st, n):
        rows, cols = tile_of(ahead(g, n))
        return to(g, ahead(g, n), s[g].at[:, rows, cols], r[g].at[st, pl.ds(5 * me[g], 5)], fwd_s.at[g, n], fwd_r.at[g, st, n])

    def fwd_own(g, st):
        rows, cols = tile_of(me[g])
        return pltpu.make_async_copy(s[g].at[:, rows, cols], r[g].at[st, pl.ds(5 * me[g], 5)], local.at[g, 0])

    def bck(g, st, n):
        rows, cols = tile_of(me[g])
        return to(g, ahead(g, n), o[g].at[pl.ds(5 * ahead(g, n), 5)], u[g].at[st, :, rows, cols], bck_s.at[g, n], bck_r.at[g, st, n])

    def bck_own(g, st):
        rows, cols = tile_of(me[g])
        return pltpu.make_async_copy(o[g].at[pl.ds(5 * me[g], 5)], u[g].at[st, :, rows, cols], local.at[g, 1])

    def fwd_start(g, st):
        loop(1, G, lambda n: fwd(g, st, n).start())
        fwd_own(g, st).start()

    def fwd_finish(g, st):
        fwd_own(g, st).wait()
        loop(1, G, lambda n: fwd(g, st, n).wait_recv())

    def bck_start(g, st):
        loop(1, G, lambda n: bck(g, st, n).start())
        bck_own(g, st).start()

    def bck_finish(g, st):
        bck_own(g, st).wait()
        loop(1, G, lambda n: bck(g, st, n).wait_recv())

    turn[...] = jnp.zeros((128, 128), F32)
    turn[0:N, 0:N] = h_in[...]
    hh, hl = split(h_in[...])
    gh, gl = split(-jnp.transpose(turn[...])[0:N, 0:N])

    def mix(g, st):
        left = (hh, hl) if g == 0 else (gh, gl)
        src = r[g].at[st].reshape(N * 16, 128)
        dst = o[g].reshape(N * 16, 128)
        for w in range(0, 16, 2):
            x = jnp.concatenate([src[pl.ds(w + e, N, stride=16), :] for e in range(2)], axis=1)
            if g == 0 and st == 1:
                x = x + time_step ** 2 / 2.0 * jnp.concatenate([dst[pl.ds(w + e, N, stride=16), :] for e in range(2)], axis=1)
            x = dot3(*left, *split(x))
            for e in range(2):
                dst[pl.ds(w + e, N, stride=16), :] = x[:, 128 * e:128 * (e + 1)]

    def rsa(g, st):
        other = pl.multiple_of(HALF * (1 - lax.rem(me[g], 2)), 8)
        return to(g, partner[g], yp[g].at[pl.ds(other, HALF)], pa[g].at[st], rsa_s.at[g], rsa_r.at[g, st])

    def rsb(g, st, n):
        rows, cols = half_piece(ahead(g, 2 * n) // 2)
        return to(g, ahead(g, 2 * n), hb[g].at[rows, cols], pb[g].at[st, n], rsb_s.at[g, n], rsb_r.at[g, st, n])

    def ag(g, st, n):
        block = yf[g].at[st, *piece(me[g])]
        return to(g, ahead(g, 2 * n), block, block, ag_s.at[g, n], ag_r.at[g, st, n])

    def ag_own(g, st):
        block = yf[g].at[st, *piece(me[g])]
        return to(g, partner[g], block, block, ag_s.at[g, 8], ag_r.at[g, st, 8])

    def ag_sent(g, st, n):
        block = yf[g].at[st, *piece(behind(g, 2 * n))]
        return to(g, ahead(g, 2 * n), block, block, ag_s.at[g, n], ag_r.at[g, st, n])

    def ag_relay(g, st, n):
        block = yf[g].at[st, *piece(behind(g, 2 * n))]
        return to(g, partner[g], block, block, ag_s.at[g, 8 + n], ag_r.at[g, st, 8 + n])

    def rsa_finish(g, st):
        rsa(g, st).wait_recv()
        keep = pl.multiple_of(HALF * lax.rem(me[g], 2), 8)
        hb[g][...] = yp[g][pl.ds(keep, HALF), :] + pa[g][st]

    zi = me[0] // 2

    def rsa_tile(st, t):
        other = pl.multiple_of(HALF * (1 - lax.rem(me[0], 2)), 8)
        cols = pl.ds(pl.multiple_of(128 * t, 128), 128)
        return to(0, partner[0], yp_r.at[pl.ds(other, HALF), cols], pa_r.at[st, :, cols], rst_s.at[t], rst_r.at[st, t])

    def turn_of(t):
        return lax.rem(zi // 2 + 1 + t, 4)

    def rsa_start(st):
        loop(0, 4, lambda t: rsa_tile(st, turn_of(t)).start())

    def rsb_start(st):
        keep = pl.multiple_of(HALF * lax.rem(me[0], 2), 8)

        def tile(t):
            t = turn_of(t)
            rsa_tile(st, t).wait_recv()
            cols = pl.ds(pl.multiple_of(128 * t, 128), 128)
            hb_r[:, cols] = yp_r[pl.ds(keep, HALF), cols] + pa_r[st, :, cols]
            for e in range(2):
                n = lax.rem(2 * t + e - zi + 8, 8)

                @pl.when(n != 0)
                def _():
                    rsb(0, st, n).start()
        loop(0, 4, tile)

    def block_of(member):
        return (
            pl.ds(pl.multiple_of(HALF * lax.rem(member, 2), 8), HALF),
            pl.ds(pl.multiple_of(128 * (member // 4), 128), 128),
        )

    def col_x(st, n):
        cols = pl.ds(pl.multiple_of(128 * (ahead(1, 4 * n) // 4), 128), 128)
        return to(1, ahead(1, 4 * n), hb_c.at[:, cols], px.at[st, n], rsb_s.at[1, n], rsb_r.at[1, st, n])

    def col_y(st):
        rows = pl.ds(pl.multiple_of(PART * (1 - low), 8), PART)
        return to(1, beside, sx.at[rows], py.at[st], rsb_s.at[1, 4], rsb_r.at[1, st, 4])

    def col_gather_y(st, member):
        block = yf_c.at[st, *piece(member)]
        return to(1, beside, block, block, ag_s.at[1, 4], ag_r.at[1, st, 4])

    def col_gather_x(st, n, member):
        block = yf_c.at[st, *block_of(member)]
        return to(1, ahead(1, 4 * n), block, block, ag_s.at[1, n], ag_r.at[1, st, n])

    def col_gather_core(st, n):
        block = yf_c.at[st, *block_of(behind(1, 4 * n))]
        return to(1, partner[1], block, block, ag_s.at[1, 8 + n], ag_r.at[1, st, 8 + n])

    def col_1(st):
        rsa_finish(1, st)
        loop(1, 4, lambda n: col_x(st, n).start())

    def col_2(st):
        loop(1, 4, lambda n: col_x(st, n).wait_recv())
        cols = pl.ds(pl.multiple_of(128 * (me[1] // 4), 128), 128)
        sx[...] = (hb_c[:, cols] + px[st, 1]) + (px[st, 2] + px[st, 3])
        col_y(st).start()

    def col_3(st):
        col_y(st).wait_recv()
        rows, cols = piece(me[1])
        total = sx[pl.ds(pl.multiple_of(PART * low, 8), PART), :] + py[st]
        yf_c[st, rows, cols] = total * v_ref[0:1, cols]
        col_gather_y(st, me[1]).start()

    def col_4(st):
        col_gather_y(st, beside).wait_recv()
        loop(1, 4, lambda n: col_gather_x(st, n, me[1]).start())
        col_gather_core(st, 0).start()

    def col_5(st):
        def relay(n):
            col_gather_x(st, n, behind(1, 4 * n)).wait_recv()
            col_gather_core(st, n).start()
        loop(1, 4, relay)

    def col_6(st):
        loop(0, 4, lambda n: col_gather_core(st, n).wait_recv())

    def col_sent(st):
        rsa(1, st).wait_send()
        loop(1, 4, lambda n: col_x(st, n).wait_send())
        col_y(st).wait_send()
        col_gather_y(st, me[1]).wait_send()
        loop(1, 4, lambda n: col_gather_x(st, n, me[1]).wait_send())
        loop(0, 4, lambda n: col_gather_core(st, n).wait_send())

    def ag_start(g, st):
        loop(1, 8, lambda n: rsb(g, st, n).wait_recv())
        rows, cols = half_piece(me[g] // 2)
        total = hb[g][rows, cols]
        for n in range(1, 8):
            total = total + pb[g][st, n]
        rows, cols = piece(me[g])
        yf[g][st, rows, cols] = total * v_ref[0:1, cols]
        loop(1, 8, lambda n: ag(g, st, n).start())
        ag_own(g, st).start()

    def relay_start(g, st):
        def relay(n):
            ag_sent(g, st, n).wait_recv()
            ag_relay(g, st, n).start()
        loop(1, 8, relay)

    def ag_finish(g, st):
        ag_own(g, st).wait_recv()
        loop(1, 8, lambda n: ag_relay(g, st, n).wait_recv())

    for p in range(B):
        for t in range(4):
            aux_in[p * 20 + t * B:p * 20 + t * B + B, :] = aux_ref[p, :, 128 * t:128 * t + 128]
    aux_in[100:PART, :] = jnp.zeros((PART - 100, 128), F32)
    enter()
    left_start(0)
    aux_start(0)
    zeros = jnp.zeros((512 - NB, 512), F32)
    wide[NB:512, :] = zeros
    start[:, 384:512] = jnp.zeros((NB, 128), F32)
    for k in range(B):
        for i in range(B):
            start[k * N:k * N + N, i * N:i * N + N] = x_in[i * N:i * N + N, k * N:k * N + N]
    pack(start, s_c)
    wide[0:NB, :] = start[...]
    stage_b[...] = jnp.transpose(wide[...])
    pack(stage_b, s_r)
    fwd_start(0, 0)
    th[...], tl[...] = split(stage_b[0:NB, :])
    xh[...], xl[...] = split(start[...])
    stage_b[NB:512, :] = zeros
    y2h[NB:512, :] = zeros.astype(BF16)
    y2l[NB:512, :] = zeros.astype(BF16)
    for g in range(2):
        yp[g][NB:2 * HALF, :] = zeros[0:2 * HALF - NB]
    v_ref[...] = jnp.broadcast_to(v_in[...].reshape(1, NAUX), (8, NAUX))
    bdh[...] = jnp.zeros((512, 512), BF16)
    bdl[...] = jnp.zeros((512, 512), BF16)
    for i in range(B):
        bdh[i * N:i * N + N, i * N:i * N + N] = hh
        bdl[i * N:i * N + N, i * N:i * N + N] = hl

    def gather_left(w, high, low):
        left_finish(w)
        for c in range(G):
            for i in range(B):
                for t in range(4):
                    stage_b[i * N + 5 * c:i * N + 5 * c + 5, 128 * t:128 * t + 128] = gathered[w][c, i * 20 + t * 5:i * 20 + t * 5 + 5, :]
        high[...], low[...] = split(stage_b[...])

    def turned_blocks():
        pick = lax.broadcasted_iota(jnp.int32, (16, N), 1) == lax.broadcasted_iota(jnp.int32, (16, N), 0) + B * me[0]
        pick = pick.astype(F32).astype(BF16)
        rows = [lax.dot_general(pick, part, NN, preferred_element_type=F32).astype(BF16) for part in (gh, gl)]
        for q in range(B):
            block = dot3(*rows, brh[q * N:q * N + N, :], brl[q * N:q * N + N, :])
            for t in range(4):
                d_in[pl.ds(t * 5 + q, 5, stride=20), :] = block[0:B, 128 * t:128 * t + 128]
        d_in[100:PART, :] = jnp.zeros((PART - 100, 128), F32)

    def gather_right():
        aux_finish(0)
        for c in range(G):
            for k in range(B):
                for t in range(4):
                    stage_b[k * N + 5 * c:k * N + 5 * c + 5, 128 * t:128 * t + 128] = a_r[c, pl.ds(t * 5 + k, 5, stride=20), :]
        brh[...], brl[...] = split(stage_b[...])

    def section(st):
        if st == 0:
            gather_left(0, blh, bll)
        if st == 0:
            yp_r[0:NB, :] = dot3(xh[...], xl[...], blh[...], bll[...])
            rsa_start(st)
            aux_relays(0)
            fwd_start(1, st)
            dloc[...] = local_terms()
            rsb_start(st)
            gather_right()
            turned_blocks()
            left_start(1)
            yp_c[0:NB, :] = dot3(th[...], tl[...], brh[...], brl[...])
            rsa(1, st).start()
            col_1(st)
            fwd_finish(0, st)
            mix(0, st)
            col_2(st)
            col_3(st)
            fwd_finish(1, st)
            mix(1, st)
            ag_start(0, st)
            col_4(st)
            bck_start(1, st)
            gather_left(1, dh, dl)
            yx[...] = dot3(xh[...], xl[...], dh[...], dl[...])
        else:
            yp_c[0:NB, :] = dot3(th[...], tl[...], brh[...], brl[...])
            rsa(1, st).start()
            dloc[...] = local_terms()
            col_1(st)
            rsb_start(st)
            col_2(st)
            fwd_finish(1, st)
            mix(1, st)
            col_3(st)
            bck_start(1, st)
            fwd_finish(0, st)
            mix(0, st)
            col_4(st)
            ag_start(0, st)
            bck_start(0, st)
        col_5(st)
        relay_start(0, st)
        bck_finish(1, st)
        unpack(u_c.at[st], wide)
        dloc[...] = dloc[...] + wide[0:NB, :]

        col_6(st)
        y2h[0:NB, :], y2l[0:NB, :] = split(yf_c[st, 0:NB, :])
        dloc[...] = dloc[...] - dot3(brh[0:NB, :], brl[0:NB, :], y2h[...], y2l[...], NT)
        ag_finish(0, st)
        f = dot3(*split(yf_r[st, 0:NB, :]), blh[...], bll[...], NT)
        dloc[...] = dloc[...] + f

        def sent():
            for g in range(1 - st, 2):
                loop(1, G, lambda n: bck(g, st, n).wait_send())
            loop(1, 8, lambda n: rsb(0, st, n).wait_send())
            loop(1, 8, lambda n: ag(0, st, n).wait_send())
            ag_own(0, st).wait_send()
            loop(1, 8, lambda n: ag_relay(0, st, n).wait_send())
            col_sent(st)

        def first_sent():
            for g in range(2):
                loop(1, G, lambda n: fwd(g, st, n).wait_send())
            loop(0, 4, lambda t: rsa_tile(st, t).wait_send())

        if st == 0:
            p = dloc[...]
            xh[...], xl[...] = split(p)
            first_sent()
            yp_r[0:NB, :] = dot3(xh[...], xl[...], blh[...], bll[...]) - yx[...]
            rsa_start(1)
            fsum[...] = start[...] + time_step * p
            wide[0:NB, :] = time_step * start[...] + (time_step ** 2 * p - time_step ** 2 / 2.0 * f)
            stage_b[0:NB, :] = jnp.transpose(wide[...])[0:NB, :]
            pack(stage_b, s_r)
            fwd_start(0, 1)
            xa[...] = p
            pack(xa, s_c)
            fwd_start(1, 1)
            wide[0:NB, :] = p
            stage_b[0:NB, :] = jnp.transpose(wide[...])[0:NB, :]
            th[...], tl[...] = split(stage_b[0:NB, :])
            sent()
            left_sent(0)
            left_sent(1)
            aux_sent(0)
        if st == 1:
            bck_finish(0, st)
            unpack(u_r.at[st], wide)
            xa[...] = (fsum[...] + time_step ** 2 / 2.0 * dloc[...]) + jnp.transpose(wide[...])[0:NB, :]
            first_sent()
            sent()
            for k in range(B):
                for i in range(B):
                    out_ref[i * N:i * N + N, k * N:k * N + N] = xa[k * N:k * N + N, i * N:i * N + N]

    def local_terms():
        left = dot3(bdh[0:NB, 0:512], bdl[0:NB, 0:512], *pad_rows())
        return left - dot3(xh[...], xl[...], bdh[...], bdl[...])

    def pad_rows():
        z = jnp.zeros((512 - NB, 512), BF16)
        return jnp.concatenate([xh[...], z], axis=0), jnp.concatenate([xl[...], z], axis=0)

    section(0)
    section(1)


def shards(pairs, one_body, aux, weights):
    vmem = pl.BlockSpec(memory_space=pltpu.VMEM)
    f32 = lambda *shape: pltpu.VMEM(shape, F32)
    b16 = lambda *shape: pltpu.VMEM(shape, BF16)
    dma = lambda *shape: pltpu.SemaphoreType.DMA(shape)
    return pl.pallas_call(
        kernel,
        out_shape=jax.ShapeDtypeStruct((NB, NB), F32),
        in_specs=[vmem] * 4,
        out_specs=vmem,
        scratch_shapes=[
            f32(NB, 512), f32(PART, 128), f32(8, NAUX), f32(128, 128),
            f32(NB, 512), b16(NB, 512), b16(NB, 512), b16(NB, 512), b16(NB, 512),
            f32(512, 512), f32(512, 512), f32(NB, 512), f32(NB, 512),
            *[b16(512, 512)] * 8,
            *[f32(B, N, 512)] * 2, *[f32(2, N, 16, 128)] * 2, *[f32(N, 16, 128)] * 2, *[f32(2, B, N, 512)] * 2,
            f32(PART, 128), f32(G, PART, 128), b16(512, 512), b16(512, 512), f32(NB, 512),
            *[f32(G, PART, 128)] * 2, *[f32(2 * HALF, 512)] * 2, *[f32(2, HALF, 512)] * 2, *[f32(HALF, 512)] * 2,
            f32(2, 8, PART, 128), f32(2, 4, HALF, 128), f32(2, PART, 128), f32(HALF, 128), *[f32(2, 2 * HALF, 512)] * 2,
            dma(2, 2), dma(3, 16), dma(3, 16), dma(2, 16), dma(2, 2, 16), dma(2, 16), dma(2, 2, 16),
            dma(2), dma(2, 2), dma(4), dma(2, 4), dma(2, 8), dma(2, 2, 8), dma(2, 16), dma(2, 2, 16),
        ],
        compiler_params=pltpu.CompilerParams(collective_id=0, has_side_effects=True, vmem_limit_bytes=60 * 1024 * 1024),
        name="heun",
    )(pairs, aux, weights, one_body)


def solution(mesh):
    in_specs = (P("row", "col"), P(), P("row", "col", None), P())
    out_specs = P("row", "col")
    return jax.shard_map(shards, mesh=mesh, in_specs=in_specs, out_specs=out_specs, check_vma=False)
```

```python
import functools

import jax
import jax.numpy as jnp
from jax import lax
from jax.experimental import pallas as pl
from jax.experimental.pallas import tpu as pltpu
from jax.sharding import PartitionSpec as P

time_step = 0.15
MESH = pl.DeviceIdType.MESH
F32, BF16 = jnp.float32, jnp.bfloat16
N, G, B, NAUX = 80, 16, 5, 512
NB = N * B
HALF, PART = 208, 104
NN = (((1,), (0,)), ((), ()))
NT = (((1,), (1,)), ((), ()))


def split(x):
    high = x.astype(BF16)
    return high, (x - high.astype(F32)).astype(BF16)


def dot3(ah, al, bh, bl, dims=NN):
    dot = functools.partial(lax.dot_general, dimension_numbers=dims, preferred_element_type=F32)
    return dot(ah, bh) + (dot(ah, bl) + dot(al, bh))


def tile_of(part):
    return pl.ds(pl.multiple_of(16 * lax.rem(part, 5), 16), 16), pl.ds(pl.multiple_of(128 * (part // 5), 128), 128)


def half_piece(z):
    return pl.ds(pl.multiple_of(PART * lax.rem(z, 2), 8), PART), pl.ds(pl.multiple_of(128 * (z // 2), 128), 128)


def piece(member):
    z = member // 2
    return (
        pl.ds(pl.multiple_of(HALF * lax.rem(member, 2) + PART * lax.rem(z, 2), 8), PART),
        pl.ds(pl.multiple_of(128 * (z // 2), 128), 128),
    )


def pack(x_ref, s_ref):
    for i in range(B):
        s_ref[i, :, 0:384] = x_ref[i * N:(i + 1) * N, 0:384]
        for lo, hi in ((0, 8), (8, 10)):
            tail = x_ref[i * N + 8 * lo:i * N + 8 * lo + 8, 384:512]
            for m in range(lo + 1, hi):
                tail = tail + pltpu.roll(x_ref[i * N + 8 * m:i * N + 8 * m + 8, 384:512], 16 * (m - lo), 1)
            s_ref[i, lo:lo + 8, 384:512] = tail


def unpack(u_ref, x_ref):
    lane = lax.broadcasted_iota(jnp.int32, (8, 128), 1)
    for i in range(B):
        x_ref[i * N:(i + 1) * N, 0:384] = u_ref[i, :, 0:384]
        for m in range(10):
            lo = 8 * (m // 8)
            tail = u_ref[i, lo:lo + 8, 384:512]
            if m % 8:
                tail = pltpu.roll(tail, 128 - 16 * (m % 8), 1)
            x_ref[i * N + 8 * m:i * N + 8 * m + 8, 384:512] = jnp.where(lane < 16, tail, 0.0)


def kernel(
    x_in, aux_ref, v_in, h_in, out_ref,
    start, aux_in, v_ref, turn,
    xa, xh, xl, th, tl, wide, stage_b, dloc, fsum,
    blh, bll, brh, brl, bdh, bdl, y2h, y2l,
    s_r, s_c, r_r, r_c, o_r, o_c, u_r, u_c,
    d_in, d_c, dh, dl, yx, a_r, a_c, yp_r, yp_c, pa_r, pa_c, hb_r, hb_c, pb_r, px, py, sx, yf_r, yf_c,
    local, aux_s, aux_r, fwd_s, fwd_r, bck_s, bck_r, rsa_s, rsa_r, rst_s, rst_r, rsb_s, rsb_r, ag_s, ag_r,
):
    me = (lax.axis_index("row"), lax.axis_index("col"))
    s, r, o, u = (s_r, s_c), (r_r, r_c), (o_r, o_c), (u_r, u_c)
    a, yp, pa, hb, pb, yf = (a_r, a_c), (yp_r, yp_c), (pa_r, pa_c), (hb_r, hb_c), (pb_r, None), (yf_r, yf_c)
    partner = tuple(m + 1 - 2 * lax.rem(m, 2) for m in me)

    def at(g, member):
        return (member, me[1]) if g == 0 else (me[0], member)

    def to(g, member, src, dst, ssem, rsem):
        return pltpu.make_async_remote_copy(
            src_ref=src, dst_ref=dst, send_sem=ssem, recv_sem=rsem, device_id=at(g, member), device_id_type=MESH
        )

    def ahead(g, n):
        return lax.rem(me[g] + n, G)

    def behind(g, n):
        return lax.rem(me[g] + G - n, G)

    def loop(lo, hi, body):
        def step(n, carry):
            body(n)
            return carry
        lax.fori_loop(lo, hi, step, 0)

    def enter():
        barrier = pltpu.get_barrier_semaphore()
        for g in range(2):
            loop(1, G, lambda n: pl.semaphore_signal(barrier, inc=1, device_id=at(g, ahead(g, n)), device_id_type=MESH))
        pl.semaphore_wait(barrier, 2 * (G - 1))

    def aux_copy(g, n):
        return to(g, ahead(g, 2 * n), aux_in, a[g].at[me[g]], aux_s.at[g, n], aux_r.at[g, n])

    def aux_relay(g, n):
        src = behind(g, 2 * n)
        block = a[g].at[src]
        return to(g, partner[g], block, block, aux_s.at[g, 8 + n], aux_r.at[g, 8 + n])

    def aux_own(g):
        return to(g, partner[g], aux_in, a[g].at[me[g]], aux_s.at[g, 8], aux_r.at[g, 8])

    def aux_start(g):
        loop(1, 8, lambda n: aux_copy(g, n).start())
        aux_own(g).start()

    def aux_relays(g):
        def relay(n):
            aux_copy(g, n).wait_recv()
            aux_relay(g, n).start()
        loop(1, 8, relay)

    def aux_finish(g):
        a[g][me[g]] = aux_in[...]
        aux_own(g).wait_recv()
        loop(1, 8, lambda n: aux_relay(g, n).wait_recv())

    def aux_sent(g):
        loop(1, 8, lambda n: aux_copy(g, n).wait_send())
        loop(1, 8, lambda n: aux_relay(g, n).wait_send())
        aux_own(g).wait_send()

    beside = me[1] + 2 - 4 * lax.rem(me[1] // 2, 2)
    low = lax.rem(me[1] // 2, 2)

    own, gathered = (aux_in, d_in), (a_c, d_c)

    def beside_of(member):
        return member + 2 - 4 * lax.rem(member // 2, 2)

    def left_y(w, member):
        return to(1, beside, own[w], gathered[w].at[member], aux_s.at[1 + w, 0], aux_r.at[1 + w, 0])

    def left_x(w, n, member):
        return to(1, ahead(1, 4 * n), own[w], gathered[w].at[member], aux_s.at[1 + w, n], aux_r.at[1 + w, n])

    def left_x2(w, n, member):
        block = gathered[w].at[member]
        return to(1, ahead(1, 4 * n), block, block, aux_s.at[1 + w, 4 + n], aux_r.at[1 + w, 4 + n])

    def left_core(w, n, member):
        block = gathered[w].at[member]
        return to(1, partner[1], block, block, aux_s.at[1 + w, 8 + n], aux_r.at[1 + w, 8 + n])

    def left_own(w):
        return to(1, partner[1], own[w], gathered[w].at[me[1]], aux_s.at[1 + w, 8], aux_r.at[1 + w, 8])

    def left_start(w):
        left_y(w, me[1]).start()
        loop(1, 4, lambda n: left_x(w, n, me[1]).start())
        left_own(w).start()

    def left_finish(w):
        gathered[w][me[1]] = own[w][...]
        left_y(w, beside).wait_recv()
        loop(1, 4, lambda n: left_x2(w, n, beside).start())
        left_core(w, 4, beside).start()

        def relay(n):
            src = behind(1, 4 * n)
            left_x(w, n, src).wait_recv()
            left_core(w, n, src).start()
        loop(1, 4, relay)

        def relay2(n):
            src = beside_of(behind(1, 4 * n))
            left_x2(w, n, src).wait_recv()
            left_core(w, 4 + n, src).start()
        loop(1, 4, relay2)
        loop(0, 8, lambda n: left_core(w, n, me[1]).wait_recv())

    def left_sent(w):
        left_y(w, me[1]).wait_send()
        loop(1, 4, lambda n: left_x(w, n, me[1]).wait_send())
        loop(1, 4, lambda n: left_x2(w, n, beside).wait_send())
        loop(0, 8, lambda n: left_core(w, n, me[1]).wait_send())

    def fwd(g, st, n):
        rows, cols = tile_of(ahead(g, n))
        return to(g, ahead(g, n), s[g].at[:, rows, cols], r[g].at[st, pl.ds(5 * me[g], 5)], fwd_s.at[g, n], fwd_r.at[g, st, n])

    def fwd_own(g, st):
        rows, cols = tile_of(me[g])
        return pltpu.make_async_copy(s[g].at[:, rows, cols], r[g].at[st, pl.ds(5 * me[g], 5)], local.at[g, 0])

    def bck(g, st, n):
        rows, cols = tile_of(me[g])
        return to(g, ahead(g, n), o[g].at[pl.ds(5 * ahead(g, n), 5)], u[g].at[st, :, rows, cols], bck_s.at[g, n], bck_r.at[g, st, n])

    def bck_own(g, st):
        rows, cols = tile_of(me[g])
        return pltpu.make_async_copy(o[g].at[pl.ds(5 * me[g], 5)], u[g].at[st, :, rows, cols], local.at[g, 1])

    def fwd_start(g, st):
        loop(1, G, lambda n: fwd(g, st, n).start())
        fwd_own(g, st).start()

    def fwd_finish(g, st):
        fwd_own(g, st).wait()
        loop(1, G, lambda n: fwd(g, st, n).wait_recv())

    def bck_start(g, st):
        loop(1, G, lambda n: bck(g, st, n).start())
        bck_own(g, st).start()

    def bck_finish(g, st):
        bck_own(g, st).wait()
        loop(1, G, lambda n: bck(g, st, n).wait_recv())

    turn[...] = jnp.zeros((128, 128), F32)
    turn[0:N, 0:N] = h_in[...]
    hh, hl = split(h_in[...])
    gh, gl = split(-jnp.transpose(turn[...])[0:N, 0:N])

    def mix(g, st):
        left = (hh, hl) if g == 0 else (gh, gl)
        src = r[g].at[st].reshape(N * 16, 128)
        dst = o[g].reshape(N * 16, 128)
        for w in range(0, 16, 2):
            x = jnp.concatenate([src[pl.ds(w + e, N, stride=16), :] for e in range(2)], axis=1)
            if g == 0 and st == 1:
                x = x + time_step ** 2 / 2.0 * jnp.concatenate([dst[pl.ds(w + e, N, stride=16), :] for e in range(2)], axis=1)
            x = dot3(*left, *split(x))
            for e in range(2):
                dst[pl.ds(w + e, N, stride=16), :] = x[:, 128 * e:128 * (e + 1)]

    def rsa(g, st):
        other = pl.multiple_of(HALF * (1 - lax.rem(me[g], 2)), 8)
        return to(g, partner[g], yp[g].at[pl.ds(other, HALF)], pa[g].at[st], rsa_s.at[g], rsa_r.at[g, st])

    def rsb(g, st, n):
        rows, cols = half_piece(ahead(g, 2 * n) // 2)
        return to(g, ahead(g, 2 * n), hb[g].at[rows, cols], pb[g].at[st, n], rsb_s.at[g, n], rsb_r.at[g, st, n])

    def ag(g, st, n):
        block = yf[g].at[st, *piece(me[g])]
        return to(g, ahead(g, 2 * n), block, block, ag_s.at[g, n], ag_r.at[g, st, n])

    def ag_own(g, st):
        block = yf[g].at[st, *piece(me[g])]
        return to(g, partner[g], block, block, ag_s.at[g, 8], ag_r.at[g, st, 8])

    def ag_sent(g, st, n):
        block = yf[g].at[st, *piece(behind(g, 2 * n))]
        return to(g, ahead(g, 2 * n), block, block, ag_s.at[g, n], ag_r.at[g, st, n])

    def ag_relay(g, st, n):
        block = yf[g].at[st, *piece(behind(g, 2 * n))]
        return to(g, partner[g], block, block, ag_s.at[g, 8 + n], ag_r.at[g, st, 8 + n])

    def rsa_finish(g, st):
        rsa(g, st).wait_recv()
        keep = pl.multiple_of(HALF * lax.rem(me[g], 2), 8)
        hb[g][...] = yp[g][pl.ds(keep, HALF), :] + pa[g][st]

    zi = me[0] // 2

    def rsa_tile(st, t):
        other = pl.multiple_of(HALF * (1 - lax.rem(me[0], 2)), 8)
        cols = pl.ds(pl.multiple_of(128 * t, 128), 128)
        return to(0, partner[0], yp_r.at[pl.ds(other, HALF), cols], pa_r.at[st, :, cols], rst_s.at[t], rst_r.at[st, t])

    def turn_of(t):
        return lax.rem(zi // 2 + 1 + t, 4)

    def rsa_start(st):
        loop(0, 4, lambda t: rsa_tile(st, turn_of(t)).start())

    def rsb_start(st):
        keep = pl.multiple_of(HALF * lax.rem(me[0], 2), 8)

        def tile(t):
            t = turn_of(t)
            rsa_tile(st, t).wait_recv()
            cols = pl.ds(pl.multiple_of(128 * t, 128), 128)
            hb_r[:, cols] = yp_r[pl.ds(keep, HALF), cols] + pa_r[st, :, cols]
            for e in range(2):
                n = lax.rem(2 * t + e - zi + 8, 8)

                @pl.when(n != 0)
                def _():
                    rsb(0, st, n).start()
        loop(0, 4, tile)

    def block_of(member):
        return (
            pl.ds(pl.multiple_of(HALF * lax.rem(member, 2), 8), HALF),
            pl.ds(pl.multiple_of(128 * (member // 4), 128), 128),
        )

    def col_x(st, n):
        cols = pl.ds(pl.multiple_of(128 * (ahead(1, 4 * n) // 4), 128), 128)
        return to(1, ahead(1, 4 * n), hb_c.at[:, cols], px.at[st, n], rsb_s.at[1, n], rsb_r.at[1, st, n])

    def col_y(st):
        rows = pl.ds(pl.multiple_of(PART * (1 - low), 8), PART)
        return to(1, beside, sx.at[rows], py.at[st], rsb_s.at[1, 4], rsb_r.at[1, st, 4])

    def col_gather_y(st, member):
        block = yf_c.at[st, *piece(member)]
        return to(1, beside, block, block, ag_s.at[1, 4], ag_r.at[1, st, 4])

    def col_gather_x(st, n, member):
        block = yf_c.at[st, *block_of(member)]
        return to(1, ahead(1, 4 * n), block, block, ag_s.at[1, n], ag_r.at[1, st, n])

    def col_gather_core(st, n):
        block = yf_c.at[st, *block_of(behind(1, 4 * n))]
        return to(1, partner[1], block, block, ag_s.at[1, 8 + n], ag_r.at[1, st, 8 + n])

    def col_1(st):
        rsa_finish(1, st)
        loop(1, 4, lambda n: col_x(st, n).start())

    def col_2(st):
        loop(1, 4, lambda n: col_x(st, n).wait_recv())
        cols = pl.ds(pl.multiple_of(128 * (me[1] // 4), 128), 128)
        sx[...] = (hb_c[:, cols] + px[st, 1]) + (px[st, 2] + px[st, 3])
        col_y(st).start()

    def col_3(st):
        col_y(st).wait_recv()
        rows, cols = piece(me[1])
        total = sx[pl.ds(pl.multiple_of(PART * low, 8), PART), :] + py[st]
        yf_c[st, rows, cols] = total * v_ref[0:1, cols]
        col_gather_y(st, me[1]).start()

    def col_4(st):
        col_gather_y(st, beside).wait_recv()
        loop(1, 4, lambda n: col_gather_x(st, n, me[1]).start())
        col_gather_core(st, 0).start()

    def col_5(st):
        def relay(n):
            col_gather_x(st, n, behind(1, 4 * n)).wait_recv()
            col_gather_core(st, n).start()
        loop(1, 4, relay)

    def col_6(st):
        loop(0, 4, lambda n: col_gather_core(st, n).wait_recv())

    def col_sent(st):
        rsa(1, st).wait_send()
        loop(1, 4, lambda n: col_x(st, n).wait_send())
        col_y(st).wait_send()
        col_gather_y(st, me[1]).wait_send()
        loop(1, 4, lambda n: col_gather_x(st, n, me[1]).wait_send())
        loop(0, 4, lambda n: col_gather_core(st, n).wait_send())

    def ag_start(g, st):
        loop(1, 8, lambda n: rsb(g, st, n).wait_recv())
        rows, cols = half_piece(me[g] // 2)
        total = hb[g][rows, cols]
        for n in range(1, 8):
            total = total + pb[g][st, n]
        rows, cols = piece(me[g])
        yf[g][st, rows, cols] = total * v_ref[0:1, cols]
        loop(1, 8, lambda n: ag(g, st, n).start())
        ag_own(g, st).start()

    def relay_start(g, st):
        def relay(n):
            ag_sent(g, st, n).wait_recv()
            ag_relay(g, st, n).start()
        loop(1, 8, relay)

    def ag_finish(g, st):
        ag_own(g, st).wait_recv()
        loop(1, 8, lambda n: ag_relay(g, st, n).wait_recv())

    for p in range(B):
        for t in range(4):
            aux_in[p * 20 + t * B:p * 20 + t * B + B, :] = aux_ref[p, :, 128 * t:128 * t + 128]
    aux_in[100:PART, :] = jnp.zeros((PART - 100, 128), F32)
    enter()
    left_start(0)
    aux_start(0)
    zeros = jnp.zeros((512 - NB, 512), F32)
    wide[NB:512, :] = zeros
    start[:, 384:512] = jnp.zeros((NB, 128), F32)
    for k in range(B):
        for i in range(B):
            start[k * N:k * N + N, i * N:i * N + N] = x_in[i * N:i * N + N, k * N:k * N + N]
    pack(start, s_c)
    wide[0:NB, :] = start[...]
    stage_b[...] = jnp.transpose(wide[...])
    pack(stage_b, s_r)
    fwd_start(0, 0)
    th[...], tl[...] = split(stage_b[0:NB, :])
    xh[...], xl[...] = split(start[...])
    stage_b[NB:512, :] = zeros
    y2h[NB:512, :] = zeros.astype(BF16)
    y2l[NB:512, :] = zeros.astype(BF16)
    for g in range(2):
        yp[g][NB:2 * HALF, :] = zeros[0:2 * HALF - NB]
    v_ref[...] = jnp.broadcast_to(v_in[...].reshape(1, NAUX), (8, NAUX))
    bdh[...] = jnp.zeros((512, 512), BF16)
    bdl[...] = jnp.zeros((512, 512), BF16)
    for i in range(B):
        bdh[i * N:i * N + N, i * N:i * N + N] = hh
        bdl[i * N:i * N + N, i * N:i * N + N] = hl

    def gather_left(w, high, low):
        left_finish(w)
        for c in range(G):
            for i in range(B):
                for t in range(4):
                    stage_b[i * N + 5 * c:i * N + 5 * c + 5, 128 * t:128 * t + 128] = gathered[w][c, i * 20 + t * 5:i * 20 + t * 5 + 5, :]
        high[...], low[...] = split(stage_b[...])

    def turned_blocks():
        pick = lax.broadcasted_iota(jnp.int32, (16, N), 1) == lax.broadcasted_iota(jnp.int32, (16, N), 0) + B * me[0]
        pick = pick.astype(F32).astype(BF16)
        rows = [lax.dot_general(pick, part, NN, preferred_element_type=F32).astype(BF16) for part in (gh, gl)]
        for q in range(B):
            block = dot3(*rows, brh[q * N:q * N + N, :], brl[q * N:q * N + N, :])
            for t in range(4):
                d_in[pl.ds(t * 5 + q, 5, stride=20), :] = block[0:B, 128 * t:128 * t + 128]
        d_in[100:PART, :] = jnp.zeros((PART - 100, 128), F32)

    def gather_right():
        aux_finish(0)
        for c in range(G):
            for k in range(B):
                for t in range(4):
                    stage_b[k * N + 5 * c:k * N + 5 * c + 5, 128 * t:128 * t + 128] = a_r[c, pl.ds(t * 5 + k, 5, stride=20), :]
        brh[...], brl[...] = split(stage_b[...])

    def section(st):
        if st == 0:
            gather_left(0, blh, bll)
        if st == 0:
            yp_r[0:NB, :] = dot3(xh[...], xl[...], blh[...], bll[...])
            rsa_start(st)
            aux_relays(0)
            fwd_start(1, st)
            dloc[...] = local_terms()
            rsb_start(st)
            gather_right()
            yp_c[0:NB, :] = dot3(th[...], tl[...], brh[...], brl[...])
            rsa(1, st).start()
            turned_blocks()
            left_start(1)
            col_1(st)
            fwd_finish(0, st)
            mix(0, st)
            col_2(st)
            col_3(st)
            fwd_finish(1, st)
            mix(1, st)
            ag_start(0, st)
            col_4(st)
            bck_start(1, st)
        else:
            yp_c[0:NB, :] = dot3(th[...], tl[...], brh[...], brl[...])
            rsa(1, st).start()
            dloc[...] = local_terms()
            col_1(st)
            rsb_start(st)
            col_2(st)
            fwd_finish(1, st)
            mix(1, st)
            col_3(st)
            bck_start(1, st)
            fwd_finish(0, st)
            mix(0, st)
            col_4(st)
            ag_start(0, st)
            bck_start(0, st)
        col_5(st)
        relay_start(0, st)
        if st == 0:
            gather_left(1, dh, dl)
            yx[...] = dot3(xh[...], xl[...], dh[...], dl[...])
        bck_finish(1, st)
        unpack(u_c.at[st], wide)
        dloc[...] = dloc[...] + wide[0:NB, :]

        col_6(st)
        y2h[0:NB, :], y2l[0:NB, :] = split(yf_c[st, 0:NB, :])
        dloc[...] = dloc[...] - dot3(brh[0:NB, :], brl[0:NB, :], y2h[...], y2l[...], NT)
        ag_finish(0, st)
        f = dot3(*split(yf_r[st, 0:NB, :]), blh[...], bll[...], NT)
        dloc[...] = dloc[...] + f

        def sent():
            for g in range(1 - st, 2):
                loop(1, G, lambda n: bck(g, st, n).wait_send())
            loop(1, 8, lambda n: rsb(0, st, n).wait_send())
            loop(1, 8, lambda n: ag(0, st, n).wait_send())
            ag_own(0, st).wait_send()
            loop(1, 8, lambda n: ag_relay(0, st, n).wait_send())
            col_sent(st)

        def first_sent():
            for g in range(2):
                loop(1, G, lambda n: fwd(g, st, n).wait_send())
            loop(0, 4, lambda t: rsa_tile(st, t).wait_send())

        if st == 0:
            p = dloc[...]
            xh[...], xl[...] = split(p)
            first_sent()
            yp_r[0:NB, :] = dot3(xh[...], xl[...], blh[...], bll[...]) - yx[...]
            rsa_start(1)
            fsum[...] = start[...] + time_step * p
            wide[0:NB, :] = time_step * start[...] + (time_step ** 2 * p - time_step ** 2 / 2.0 * f)
            stage_b[0:NB, :] = jnp.transpose(wide[...])[0:NB, :]
            pack(stage_b, s_r)
            fwd_start(0, 1)
            xa[...] = p
            pack(xa, s_c)
            fwd_start(1, 1)
            wide[0:NB, :] = p
            stage_b[0:NB, :] = jnp.transpose(wide[...])[0:NB, :]
            th[...], tl[...] = split(stage_b[0:NB, :])
            sent()
            left_sent(0)
            left_sent(1)
            aux_sent(0)
        if st == 1:
            bck_finish(0, st)
            unpack(u_r.at[st], wide)
            xa[...] = (fsum[...] + time_step ** 2 / 2.0 * dloc[...]) + jnp.transpose(wide[...])[0:NB, :]
            first_sent()
            sent()
            for k in range(B):
                for i in range(B):
                    out_ref[i * N:i * N + N, k * N:k * N + N] = xa[k * N:k * N + N, i * N:i * N + N]

    def local_terms():
        left = dot3(bdh[0:NB, 0:512], bdl[0:NB, 0:512], *pad_rows())
        return left - dot3(xh[...], xl[...], bdh[...], bdl[...])

    def pad_rows():
        z = jnp.zeros((512 - NB, 512), BF16)
        return jnp.concatenate([xh[...], z], axis=0), jnp.concatenate([xl[...], z], axis=0)

    section(0)
    section(1)


def shards(pairs, one_body, aux, weights):
    vmem = pl.BlockSpec(memory_space=pltpu.VMEM)
    f32 = lambda *shape: pltpu.VMEM(shape, F32)
    b16 = lambda *shape: pltpu.VMEM(shape, BF16)
    dma = lambda *shape: pltpu.SemaphoreType.DMA(shape)
    return pl.pallas_call(
        kernel,
        out_shape=jax.ShapeDtypeStruct((NB, NB), F32),
        in_specs=[vmem] * 4,
        out_specs=vmem,
        scratch_shapes=[
            f32(NB, 512), f32(PART, 128), f32(8, NAUX), f32(128, 128),
            f32(NB, 512), b16(NB, 512), b16(NB, 512), b16(NB, 512), b16(NB, 512),
            f32(512, 512), f32(512, 512), f32(NB, 512), f32(NB, 512),
            *[b16(512, 512)] * 8,
            *[f32(B, N, 512)] * 2, *[f32(2, N, 16, 128)] * 2, *[f32(N, 16, 128)] * 2, *[f32(2, B, N, 512)] * 2,
            f32(PART, 128), f32(G, PART, 128), b16(512, 512), b16(512, 512), f32(NB, 512),
            *[f32(G, PART, 128)] * 2, *[f32(2 * HALF, 512)] * 2, *[f32(2, HALF, 512)] * 2, *[f32(HALF, 512)] * 2,
            f32(2, 8, PART, 128), f32(2, 4, HALF, 128), f32(2, PART, 128), f32(HALF, 128), *[f32(2, 2 * HALF, 512)] * 2,
            dma(2, 2), dma(3, 16), dma(3, 16), dma(2, 16), dma(2, 2, 16), dma(2, 16), dma(2, 2, 16),
            dma(2), dma(2, 2), dma(4), dma(2, 4), dma(2, 8), dma(2, 2, 8), dma(2, 16), dma(2, 2, 16),
        ],
        compiler_params=pltpu.CompilerParams(collective_id=0, has_side_effects=True, vmem_limit_bytes=60 * 1024 * 1024),
        name="heun",
    )(pairs, aux, weights, one_body)


def solution(mesh):
    in_specs = (P("row", "col"), P(), P("row", "col", None), P())
    out_specs = P("row", "col")
    return jax.shard_map(shards, mesh=mesh, in_specs=in_specs, out_specs=out_specs, check_vma=False)
```

```python
import functools

import jax
import jax.numpy as jnp
from jax import lax
from jax.experimental import pallas as pl
from jax.experimental.pallas import tpu as pltpu
from jax.sharding import PartitionSpec as P

time_step = 0.15
MESH = pl.DeviceIdType.MESH
F32, BF16 = jnp.float32, jnp.bfloat16
N, G, B, NAUX = 80, 16, 5, 512
NB = N * B
HALF, PART = 208, 104
NN = (((1,), (0,)), ((), ()))
NT = (((1,), (1,)), ((), ()))


def split(x):
    high = x.astype(BF16)
    return high, (x - high.astype(F32)).astype(BF16)


def dot3(ah, al, bh, bl, dims=NN):
    dot = functools.partial(lax.dot_general, dimension_numbers=dims, preferred_element_type=F32)
    return dot(ah, bh) + (dot(ah, bl) + dot(al, bh))


def tile_of(part):
    return pl.ds(pl.multiple_of(16 * lax.rem(part, 5), 16), 16), pl.ds(pl.multiple_of(128 * (part // 5), 128), 128)


def half_piece(z):
    return pl.ds(pl.multiple_of(PART * lax.rem(z, 2), 8), PART), pl.ds(pl.multiple_of(128 * (z // 2), 128), 128)


def piece(member):
    z = member // 2
    return (
        pl.ds(pl.multiple_of(HALF * lax.rem(member, 2) + PART * lax.rem(z, 2), 8), PART),
        pl.ds(pl.multiple_of(128 * (z // 2), 128), 128),
    )


def pack(x_ref, s_ref):
    for i in range(B):
        s_ref[i, :, 0:384] = x_ref[i * N:(i + 1) * N, 0:384]
        for lo, hi in ((0, 8), (8, 10)):
            tail = x_ref[i * N + 8 * lo:i * N + 8 * lo + 8, 384:512]
            for m in range(lo + 1, hi):
                tail = tail + pltpu.roll(x_ref[i * N + 8 * m:i * N + 8 * m + 8, 384:512], 16 * (m - lo), 1)
            s_ref[i, lo:lo + 8, 384:512] = tail


def unpack(u_ref, x_ref):
    lane = lax.broadcasted_iota(jnp.int32, (8, 128), 1)
    for i in range(B):
        x_ref[i * N:(i + 1) * N, 0:384] = u_ref[i, :, 0:384]
        for m in range(10):
            lo = 8 * (m // 8)
            tail = u_ref[i, lo:lo + 8, 384:512]
            if m % 8:
                tail = pltpu.roll(tail, 128 - 16 * (m % 8), 1)
            x_ref[i * N + 8 * m:i * N + 8 * m + 8, 384:512] = jnp.where(lane < 16, tail, 0.0)


def kernel(
    x_in, aux_ref, v_in, h_in, out_ref,
    start, aux_in, v_ref, turn,
    xa, xh, xl, th, tl, wide, stage_b, dloc, fsum,
    blh, bll, brh, brl, bdh, bdl, y2h, y2l,
    s_r, s_c, r_r, r_c, o_r, o_c, u_r, u_c,
    d_in, d_c, dh, dl, yx, a_r, a_c, yp_r, yp_c, pa_r, pa_c, hb_r, hb_c, pb_r, px, py, sx, yf_r, yf_c,
    local, aux_s, aux_r, fwd_s, fwd_r, bck_s, bck_r, rsa_s, rsa_r, rst_s, rst_r, rsb_s, rsb_r, ag_s, ag_r,
):
    me = (lax.axis_index("row"), lax.axis_index("col"))
    s, r, o, u = (s_r, s_c), (r_r, r_c), (o_r, o_c), (u_r, u_c)
    a, yp, pa, hb, pb, yf = (a_r, a_c), (yp_r, yp_c), (pa_r, pa_c), (hb_r, hb_c), (pb_r, None), (yf_r, yf_c)
    partner = tuple(m + 1 - 2 * lax.rem(m, 2) for m in me)

    def at(g, member):
        return (member, me[1]) if g == 0 else (me[0], member)

    def to(g, member, src, dst, ssem, rsem):
        return pltpu.make_async_remote_copy(
            src_ref=src, dst_ref=dst, send_sem=ssem, recv_sem=rsem, device_id=at(g, member), device_id_type=MESH
        )

    def ahead(g, n):
        return lax.rem(me[g] + n, G)

    def behind(g, n):
        return lax.rem(me[g] + G - n, G)

    def loop(lo, hi, body):
        def step(n, carry):
            body(n)
            return carry
        lax.fori_loop(lo, hi, step, 0)

    def enter():
        barrier = pltpu.get_barrier_semaphore()
        for g in range(2):
            loop(1, G, lambda n: pl.semaphore_signal(barrier, inc=1, device_id=at(g, ahead(g, n)), device_id_type=MESH))
        pl.semaphore_wait(barrier, 2 * (G - 1))

    def aux_copy(g, n):
        return to(g, ahead(g, 2 * n), aux_in, a[g].at[me[g]], aux_s.at[g, n], aux_r.at[g, n])

    def aux_relay(g, n):
        src = behind(g, 2 * n)
        block = a[g].at[src]
        return to(g, partner[g], block, block, aux_s.at[g, 8 + n], aux_r.at[g, 8 + n])

    def aux_own(g):
        return to(g, partner[g], aux_in, a[g].at[me[g]], aux_s.at[g, 8], aux_r.at[g, 8])

    def aux_start(g):
        loop(1, 8, lambda n: aux_copy(g, n).start())
        aux_own(g).start()

    def aux_relays(g):
        def relay(n):
            aux_copy(g, n).wait_recv()
            aux_relay(g, n).start()
        loop(1, 8, relay)

    def aux_finish(g):
        a[g][me[g]] = aux_in[...]
        aux_own(g).wait_recv()
        loop(1, 8, lambda n: aux_relay(g, n).wait_recv())

    def aux_sent(g):
        loop(1, 8, lambda n: aux_copy(g, n).wait_send())
        loop(1, 8, lambda n: aux_relay(g, n).wait_send())
        aux_own(g).wait_send()

    beside = me[1] + 2 - 4 * lax.rem(me[1] // 2, 2)
    low = lax.rem(me[1] // 2, 2)

    own, gathered = (aux_in, d_in), (a_c, d_c)

    def beside_of(member):
        return member + 2 - 4 * lax.rem(member // 2, 2)

    def left_y(w, member):
        return to(1, beside, own[w], gathered[w].at[member], aux_s.at[1 + w, 0], aux_r.at[1 + w, 0])

    def left_x(w, n, member):
        return to(1, ahead(1, 4 * n), own[w], gathered[w].at[member], aux_s.at[1 + w, n], aux_r.at[1 + w, n])

    def left_x2(w, n, member):
        block = gathered[w].at[member]
        return to(1, ahead(1, 4 * n), block, block, aux_s.at[1 + w, 4 + n], aux_r.at[1 + w, 4 + n])

    def left_core(w, n, member):
        block = gathered[w].at[member]
        return to(1, partner[1], block, block, aux_s.at[1 + w, 8 + n], aux_r.at[1 + w, 8 + n])

    def left_own(w):
        return to(1, partner[1], own[w], gathered[w].at[me[1]], aux_s.at[1 + w, 8], aux_r.at[1 + w, 8])

    def left_start(w):
        left_y(w, me[1]).start()
        loop(1, 4, lambda n: left_x(w, n, me[1]).start())
        left_own(w).start()

    def left_finish(w):
        gathered[w][me[1]] = own[w][...]
        left_y(w, beside).wait_recv()
        loop(1, 4, lambda n: left_x2(w, n, beside).start())
        left_core(w, 4, beside).start()

        def relay(n):
            src = behind(1, 4 * n)
            left_x(w, n, src).wait_recv()
            left_core(w, n, src).start()
        loop(1, 4, relay)

        def relay2(n):
            src = beside_of(behind(1, 4 * n))
            left_x2(w, n, src).wait_recv()
            left_core(w, 4 + n, src).start()
        loop(1, 4, relay2)
        loop(0, 8, lambda n: left_core(w, n, me[1]).wait_recv())

    def left_sent(w):
        left_y(w, me[1]).wait_send()
        loop(1, 4, lambda n: left_x(w, n, me[1]).wait_send())
        loop(1, 4, lambda n: left_x2(w, n, beside).wait_send())
        loop(0, 8, lambda n: left_core(w, n, me[1]).wait_send())

    def fwd(g, st, n):
        rows, cols = tile_of(ahead(g, n))
        return to(g, ahead(g, n), s[g].at[:, rows, cols], r[g].at[st, pl.ds(5 * me[g], 5)], fwd_s.at[g, n], fwd_r.at[g, st, n])

    def fwd_own(g, st):
        rows, cols = tile_of(me[g])
        return pltpu.make_async_copy(s[g].at[:, rows, cols], r[g].at[st, pl.ds(5 * me[g], 5)], local.at[g, 0])

    def bck(g, st, n):
        rows, cols = tile_of(me[g])
        return to(g, ahead(g, n), o[g].at[pl.ds(5 * ahead(g, n), 5)], u[g].at[st, :, rows, cols], bck_s.at[g, n], bck_r.at[g, st, n])

    def bck_own(g, st):
        rows, cols = tile_of(me[g])
        return pltpu.make_async_copy(o[g].at[pl.ds(5 * me[g], 5)], u[g].at[st, :, rows, cols], local.at[g, 1])

    def fwd_start(g, st):
        loop(1, G, lambda n: fwd(g, st, n).start())
        fwd_own(g, st).start()

    def fwd_finish(g, st):
        fwd_own(g, st).wait()
        loop(1, G, lambda n: fwd(g, st, n).wait_recv())

    def bck_start(g, st):
        loop(1, G, lambda n: bck(g, st, n).start())
        bck_own(g, st).start()

    def bck_finish(g, st):
        bck_own(g, st).wait()
        loop(1, G, lambda n: bck(g, st, n).wait_recv())

    turn[...] = jnp.zeros((128, 128), F32)
    turn[0:N, 0:N] = h_in[...]
    hh, hl = split(h_in[...])
    gh, gl = split(-jnp.transpose(turn[...])[0:N, 0:N])

    def mix(g, st):
        left = (hh, hl) if g == 0 else (gh, gl)
        src = r[g].at[st].reshape(N * 16, 128)
        dst = o[g].reshape(N * 16, 128)
        for w in range(0, 16, 2):
            x = jnp.concatenate([src[pl.ds(w + e, N, stride=16), :] for e in range(2)], axis=1)
            if g == 0 and st == 1:
                x = x + time_step ** 2 / 2.0 * jnp.concatenate([dst[pl.ds(w + e, N, stride=16), :] for e in range(2)], axis=1)
            x = dot3(*left, *split(x))
            for e in range(2):
                dst[pl.ds(w + e, N, stride=16), :] = x[:, 128 * e:128 * (e + 1)]

    def rsa(g, st):
        other = pl.multiple_of(HALF * (1 - lax.rem(me[g], 2)), 8)
        return to(g, partner[g], yp[g].at[pl.ds(other, HALF)], pa[g].at[st], rsa_s.at[g], rsa_r.at[g, st])

    def rsb(g, st, n):
        rows, cols = half_piece(ahead(g, 2 * n) // 2)
        return to(g, ahead(g, 2 * n), hb[g].at[rows, cols], pb[g].at[st, n], rsb_s.at[g, n], rsb_r.at[g, st, n])

    def ag(g, st, n):
        block = yf[g].at[st, *piece(me[g])]
        return to(g, ahead(g, 2 * n), block, block, ag_s.at[g, n], ag_r.at[g, st, n])

    def ag_own(g, st):
        block = yf[g].at[st, *piece(me[g])]
        return to(g, partner[g], block, block, ag_s.at[g, 8], ag_r.at[g, st, 8])

    def ag_sent(g, st, n):
        block = yf[g].at[st, *piece(behind(g, 2 * n))]
        return to(g, ahead(g, 2 * n), block, block, ag_s.at[g, n], ag_r.at[g, st, n])

    def ag_relay(g, st, n):
        block = yf[g].at[st, *piece(behind(g, 2 * n))]
        return to(g, partner[g], block, block, ag_s.at[g, 8 + n], ag_r.at[g, st, 8 + n])

    def rsa_finish(g, st):
        rsa(g, st).wait_recv()
        keep = pl.multiple_of(HALF * lax.rem(me[g], 2), 8)
        hb[g][...] = yp[g][pl.ds(keep, HALF), :] + pa[g][st]

    zi = me[0] // 2

    def rsa_tile(st, t):
        other = pl.multiple_of(HALF * (1 - lax.rem(me[0], 2)), 8)
        cols = pl.ds(pl.multiple_of(128 * t, 128), 128)
        return to(0, partner[0], yp_r.at[pl.ds(other, HALF), cols], pa_r.at[st, :, cols], rst_s.at[t], rst_r.at[st, t])

    def turn_of(t):
        return lax.rem(zi // 2 + 1 + t, 4)

    def rsa_start(st):
        loop(0, 4, lambda t: rsa_tile(st, turn_of(t)).start())

    def rsb_start(st):
        keep = pl.multiple_of(HALF * lax.rem(me[0], 2), 8)

        def tile(t):
            t = turn_of(t)
            rsa_tile(st, t).wait_recv()
            cols = pl.ds(pl.multiple_of(128 * t, 128), 128)
            hb_r[:, cols] = yp_r[pl.ds(keep, HALF), cols] + pa_r[st, :, cols]
            for e in range(2):
                n = lax.rem(2 * t + e - zi + 8, 8)

                @pl.when(n != 0)
                def _():
                    rsb(0, st, n).start()
        loop(0, 4, tile)

    def block_of(member):
        return (
            pl.ds(pl.multiple_of(HALF * lax.rem(member, 2), 8), HALF),
            pl.ds(pl.multiple_of(128 * (member // 4), 128), 128),
        )

    def col_x(st, n):
        cols = pl.ds(pl.multiple_of(128 * (ahead(1, 4 * n) // 4), 128), 128)
        return to(1, ahead(1, 4 * n), hb_c.at[:, cols], px.at[st, n], rsb_s.at[1, n], rsb_r.at[1, st, n])

    def col_y(st):
        rows = pl.ds(pl.multiple_of(PART * (1 - low), 8), PART)
        return to(1, beside, sx.at[rows], py.at[st], rsb_s.at[1, 4], rsb_r.at[1, st, 4])

    def col_gather_y(st, member):
        block = yf_c.at[st, *piece(member)]
        return to(1, beside, block, block, ag_s.at[1, 4], ag_r.at[1, st, 4])

    def col_gather_x(st, n, member):
        block = yf_c.at[st, *block_of(member)]
        return to(1, ahead(1, 4 * n), block, block, ag_s.at[1, n], ag_r.at[1, st, n])

    def col_gather_core(st, n):
        block = yf_c.at[st, *block_of(behind(1, 4 * n))]
        return to(1, partner[1], block, block, ag_s.at[1, 8 + n], ag_r.at[1, st, 8 + n])

    def col_1(st):
        rsa_finish(1, st)
        loop(1, 4, lambda n: col_x(st, n).start())

    def col_2(st):
        loop(1, 4, lambda n: col_x(st, n).wait_recv())
        cols = pl.ds(pl.multiple_of(128 * (me[1] // 4), 128), 128)
        sx[...] = (hb_c[:, cols] + px[st, 1]) + (px[st, 2] + px[st, 3])
        col_y(st).start()

    def col_3(st):
        col_y(st).wait_recv()
        rows, cols = piece(me[1])
        total = sx[pl.ds(pl.multiple_of(PART * low, 8), PART), :] + py[st]
        yf_c[st, rows, cols] = total * v_ref[0:1, cols]
        col_gather_y(st, me[1]).start()

    def col_4(st):
        col_gather_y(st, beside).wait_recv()
        loop(1, 4, lambda n: col_gather_x(st, n, me[1]).start())
        col_gather_core(st, 0).start()

    def col_5(st):
        def relay(n):
            col_gather_x(st, n, behind(1, 4 * n)).wait_recv()
            col_gather_core(st, n).start()
        loop(1, 4, relay)

    def col_6(st):
        loop(0, 4, lambda n: col_gather_core(st, n).wait_recv())

    def col_sent(st):
        rsa(1, st).wait_send()
        loop(1, 4, lambda n: col_x(st, n).wait_send())
        col_y(st).wait_send()
        col_gather_y(st, me[1]).wait_send()
        loop(1, 4, lambda n: col_gather_x(st, n, me[1]).wait_send())
        loop(0, 4, lambda n: col_gather_core(st, n).wait_send())

    def ag_start(g, st):
        loop(1, 8, lambda n: rsb(g, st, n).wait_recv())
        rows, cols = half_piece(me[g] // 2)
        total = hb[g][rows, cols]
        for n in range(1, 8):
            total = total + pb[g][st, n]
        rows, cols = piece(me[g])
        yf[g][st, rows, cols] = total * v_ref[0:1, cols]
        loop(1, 8, lambda n: ag(g, st, n).start())
        ag_own(g, st).start()

    def relay_start(g, st):
        def relay(n):
            ag_sent(g, st, n).wait_recv()
            ag_relay(g, st, n).start()
        loop(1, 8, relay)

    def ag_finish(g, st):
        ag_own(g, st).wait_recv()
        loop(1, 8, lambda n: ag_relay(g, st, n).wait_recv())

    for p in range(B):
        for t in range(4):
            aux_in[p * 20 + t * B:p * 20 + t * B + B, :] = aux_ref[p, :, 128 * t:128 * t + 128]
    aux_in[100:PART, :] = jnp.zeros((PART - 100, 128), F32)
    enter()
    left_start(0)
    aux_start(0)
    zeros = jnp.zeros((512 - NB, 512), F32)
    wide[NB:512, :] = zeros
    start[:, 384:512] = jnp.zeros((NB, 128), F32)
    for k in range(B):
        for i in range(B):
            start[k * N:k * N + N, i * N:i * N + N] = x_in[i * N:i * N + N, k * N:k * N + N]
    pack(start, s_c)
    wide[0:NB, :] = start[...]
    stage_b[...] = jnp.transpose(wide[...])
    pack(stage_b, s_r)
    fwd_start(0, 0)
    th[...], tl[...] = split(stage_b[0:NB, :])
    xh[...], xl[...] = split(start[...])
    stage_b[NB:512, :] = zeros
    y2h[NB:512, :] = zeros.astype(BF16)
    y2l[NB:512, :] = zeros.astype(BF16)
    for g in range(2):
        yp[g][NB:2 * HALF, :] = zeros[0:2 * HALF - NB]
    v_ref[...] = jnp.broadcast_to(v_in[...].reshape(1, NAUX), (8, NAUX))
    bdh[...] = jnp.zeros((512, 512), BF16)
    bdl[...] = jnp.zeros((512, 512), BF16)
    for i in range(B):
        bdh[i * N:i * N + N, i * N:i * N + N] = hh
        bdl[i * N:i * N + N, i * N:i * N + N] = hl

    def gather_left(w, high, low):
        left_finish(w)
        if w == 0:
            aux_relays(0)
        for c in range(G):
            for i in range(B):
                for t in range(4):
                    stage_b[i * N + 5 * c:i * N + 5 * c + 5, 128 * t:128 * t + 128] = gathered[w][c, i * 20 + t * 5:i * 20 + t * 5 + 5, :]
        high[...], low[...] = split(stage_b[...])

    def turned_blocks():
        pick = lax.broadcasted_iota(jnp.int32, (16, N), 1) == lax.broadcasted_iota(jnp.int32, (16, N), 0) + B * me[0]
        pick = pick.astype(F32).astype(BF16)
        rows = [lax.dot_general(pick, part, NN, preferred_element_type=F32).astype(BF16) for part in (gh, gl)]
        for q in range(B):
            block = dot3(*rows, brh[q * N:q * N + N, :], brl[q * N:q * N + N, :])
            for t in range(4):
                d_in[pl.ds(t * 5 + q, 5, stride=20), :] = block[0:B, 128 * t:128 * t + 128]
        d_in[100:PART, :] = jnp.zeros((PART - 100, 128), F32)

    def gather_right():
        aux_finish(0)
        for c in range(G):
            for k in range(B):
                for t in range(4):
                    stage_b[k * N + 5 * c:k * N + 5 * c + 5, 128 * t:128 * t + 128] = a_r[c, pl.ds(t * 5 + k, 5, stride=20), :]
        brh[...], brl[...] = split(stage_b[...])

    def section(st):
        if st == 0:
            gather_left(0, blh, bll)
        if st == 0:
            yp_r[0:NB, :] = dot3(xh[...], xl[...], blh[...], bll[...])
            rsa_start(st)
            fwd_start(1, st)
            dloc[...] = local_terms()
            rsb_start(st)
            gather_right()
            yp_c[0:NB, :] = dot3(th[...], tl[...], brh[...], brl[...])
            rsa(1, st).start()
            turned_blocks()
            left_start(1)
            col_1(st)
            fwd_finish(0, st)
            mix(0, st)
            col_2(st)
            col_3(st)
            fwd_finish(1, st)
            mix(1, st)
            ag_start(0, st)
            col_4(st)
            bck_start(1, st)
        else:
            yp_c[0:NB, :] = dot3(th[...], tl[...], brh[...], brl[...])
            rsa(1, st).start()
            dloc[...] = local_terms()
            col_1(st)
            rsb_start(st)
            col_2(st)
            fwd_finish(1, st)
            mix(1, st)
            col_3(st)
            bck_start(1, st)
            fwd_finish(0, st)
            mix(0, st)
            col_4(st)
            ag_start(0, st)
            bck_start(0, st)
        col_5(st)
        relay_start(0, st)
        if st == 0:
            gather_left(1, dh, dl)
            yx[...] = dot3(xh[...], xl[...], dh[...], dl[...])
        bck_finish(1, st)
        unpack(u_c.at[st], wide)
        dloc[...] = dloc[...] + wide[0:NB, :]

        col_6(st)
        y2h[0:NB, :], y2l[0:NB, :] = split(yf_c[st, 0:NB, :])
        dloc[...] = dloc[...] - dot3(brh[0:NB, :], brl[0:NB, :], y2h[...], y2l[...], NT)
        ag_finish(0, st)
        f = dot3(*split(yf_r[st, 0:NB, :]), blh[...], bll[...], NT)
        dloc[...] = dloc[...] + f

        def sent():
            for g in range(1 - st, 2):
                loop(1, G, lambda n: bck(g, st, n).wait_send())
            loop(1, 8, lambda n: rsb(0, st, n).wait_send())
            loop(1, 8, lambda n: ag(0, st, n).wait_send())
            ag_own(0, st).wait_send()
            loop(1, 8, lambda n: ag_relay(0, st, n).wait_send())
            col_sent(st)

        def first_sent():
            for g in range(2):
                loop(1, G, lambda n: fwd(g, st, n).wait_send())
            loop(0, 4, lambda t: rsa_tile(st, t).wait_send())

        if st == 0:
            p = dloc[...]
            xh[...], xl[...] = split(p)
            first_sent()
            yp_r[0:NB, :] = dot3(xh[...], xl[...], blh[...], bll[...]) - yx[...]
            rsa_start(1)
            fsum[...] = start[...] + time_step * p
            wide[0:NB, :] = time_step * start[...] + (time_step ** 2 * p - time_step ** 2 / 2.0 * f)
            stage_b[0:NB, :] = jnp.transpose(wide[...])[0:NB, :]
            pack(stage_b, s_r)
            fwd_start(0, 1)
            xa[...] = p
            pack(xa, s_c)
            fwd_start(1, 1)
            wide[0:NB, :] = p
            stage_b[0:NB, :] = jnp.transpose(wide[...])[0:NB, :]
            th[...], tl[...] = split(stage_b[0:NB, :])
            sent()
            left_sent(0)
            left_sent(1)
            aux_sent(0)
        if st == 1:
            bck_finish(0, st)
            unpack(u_r.at[st], wide)
            xa[...] = (fsum[...] + time_step ** 2 / 2.0 * dloc[...]) + jnp.transpose(wide[...])[0:NB, :]
            first_sent()
            sent()
            for k in range(B):
                for i in range(B):
                    out_ref[i * N:i * N + N, k * N:k * N + N] = xa[k * N:k * N + N, i * N:i * N + N]

    def local_terms():
        left = dot3(bdh[0:NB, 0:512], bdl[0:NB, 0:512], *pad_rows())
        return left - dot3(xh[...], xl[...], bdh[...], bdl[...])

    def pad_rows():
        z = jnp.zeros((512 - NB, 512), BF16)
        return jnp.concatenate([xh[...], z], axis=0), jnp.concatenate([xl[...], z], axis=0)

    section(0)
    section(1)


def shards(pairs, one_body, aux, weights):
    vmem = pl.BlockSpec(memory_space=pltpu.VMEM)
    f32 = lambda *shape: pltpu.VMEM(shape, F32)
    b16 = lambda *shape: pltpu.VMEM(shape, BF16)
    dma = lambda *shape: pltpu.SemaphoreType.DMA(shape)
    return pl.pallas_call(
        kernel,
        out_shape=jax.ShapeDtypeStruct((NB, NB), F32),
        in_specs=[vmem] * 4,
        out_specs=vmem,
        scratch_shapes=[
            f32(NB, 512), f32(PART, 128), f32(8, NAUX), f32(128, 128),
            f32(NB, 512), b16(NB, 512), b16(NB, 512), b16(NB, 512), b16(NB, 512),
            f32(512, 512), f32(512, 512), f32(NB, 512), f32(NB, 512),
            *[b16(512, 512)] * 8,
            *[f32(B, N, 512)] * 2, *[f32(2, N, 16, 128)] * 2, *[f32(N, 16, 128)] * 2, *[f32(2, B, N, 512)] * 2,
            f32(PART, 128), f32(G, PART, 128), b16(512, 512), b16(512, 512), f32(NB, 512),
            *[f32(G, PART, 128)] * 2, *[f32(2 * HALF, 512)] * 2, *[f32(2, HALF, 512)] * 2, *[f32(HALF, 512)] * 2,
            f32(2, 8, PART, 128), f32(2, 4, HALF, 128), f32(2, PART, 128), f32(HALF, 128), *[f32(2, 2 * HALF, 512)] * 2,
            dma(2, 2), dma(3, 16), dma(3, 16), dma(2, 16), dma(2, 2, 16), dma(2, 16), dma(2, 2, 16),
            dma(2), dma(2, 2), dma(4), dma(2, 4), dma(2, 8), dma(2, 2, 8), dma(2, 16), dma(2, 2, 16),
        ],
        compiler_params=pltpu.CompilerParams(collective_id=0, has_side_effects=True, vmem_limit_bytes=60 * 1024 * 1024),
        name="heun",
    )(pairs, aux, weights, one_body)


def solution(mesh):
    in_specs = (P("row", "col"), P(), P("row", "col", None), P())
    out_specs = P("row", "col")
    return jax.shard_map(shards, mesh=mesh, in_specs=in_specs, out_specs=out_specs, check_vma=False)
```
